32 devices in a mesh: ctx: 8 (over z, x), heads: 4 (over y, core).
Axes of the slice: x: 2, y: 2, z: 4, core: 2. Of those that a mesh axis runs over, the one named last changes fastest.
Arguments:
- activations: bfloat16 [2048, 8192], P('ctx', 'heads'), may hold values from -20 to 20
- w_query: bfloat16 [8192, 4096], P(None, 'heads'), may hold values from -0.0625 to 0.0625
- w_key: bfloat16 [8192, 1024], P(None, 'heads'), may hold values from -0.0625 to 0.0625
- w_value: bfloat16 [8192, 1024], P(None, 'heads'), may hold values from -0.0625 to 0.0625
- doc_lengths: int32 [8], replicated, may hold values from 1 to 1024, 2048 in all
- block_dest: int32 [32], replicated, may hold values from 0 to 7, as said below
- out_grad: bfloat16 [2048, 4096], P('ctx', 'heads'), may hold values from -6 to 6
Outputs:
- attention: bfloat16 [2048, 4096], P('ctx', 'heads')
- input_grad: bfloat16 [2048, 8192], P('ctx', 'heads')
The draws below stay inside these ranges and needn't reach their ends.
Inputs may be any that keep to these rules, and one draw needn't show every extreme that they name: `block_dest`: loader block b lies on loader shard b // 4. Each loader shard sends its blocks to different context shards, and each context shard receives exactly 4 blocks, from different loader shards.
All inputs are finite; a program needn't handle non-finite values.
Results may differ from the reference program's by a relative error of at most 0.025.
The reference program's roundings to bfloat16 on the way count: a program that leaves them out, or rounds other values in their place, can miss the bound.
Values may be sent and summed in bfloat16 or wider, within the bound.
A program may use at most 128 MiB of HBM per device.

```python
import math
import jax
import jax.numpy as jnp
import numpy as np
from jax import lax

D = 8192
KVH = 8
HD = 128
QPK = 4
NDOC = 8
TOK_DEV = 256
BLK = 64
TOKENS = 2048
QH = 32


def draw_activations(key, part):
    entries = jnp.clip(jax.random.normal(key, (TOKENS, D), jnp.float32), -6.0, 6.0)
    return entries.astype(jnp.bfloat16)


def draw_block_dest(key, part):
    shards = TOKENS // TOK_DEV
    blocks_each = TOK_DEV // BLK
    first, second, third = jax.random.split(jax.random.fold_in(key, 17), 3)
    perm_rows = jax.random.permutation(first, shards).astype(jnp.int32)
    perm_cols = jax.random.permutation(second, shards).astype(jnp.int32)
    offsets = jax.random.permutation(third, shards).astype(jnp.int32)[:blocks_each]
    cells = jnp.mod(perm_rows[:, None] + offsets[None, :], shards)
    return perm_cols[cells].reshape(-1).astype(jnp.int32)


def shard_levels(key, extent, pieces, low, high):
    level = 1.0
    for dim, blocks in pieces:
        steps = jax.random.uniform(jax.random.fold_in(jax.random.fold_in(key, 6), dim), (blocks,), jnp.float32, low / len(pieces), high / len(pieces))
        level = level * jnp.repeat(jnp.exp(steps), extent[dim] // blocks).reshape((-1,) + (1,) * (len(extent) - 1 - dim))
    return level


def length_profile(count, total, reach, skew):
    loads = [(1 << 20) // math.isqrt(standing ** skew) + 1 for standing in range(2, count + 1)]
    spare, holding = total - reach - (count - 1), [1] * (count - 1)
    while spare > 0:
        free = [i for i in range(count - 1) if holding[i] < reach]
        whole, budget = sum([loads[i] for i in free]), spare
        for i in free:
            extra = min(reach - holding[i], max(1, budget * loads[i] // whole), spare)
            holding[i] = holding[i] + extra
            spare = spare - extra
    return np.array([reach] + holding)


def ragged(own_key, number_of, total, limit, lean):
    if number_of == 2:
        one = jax.random.randint(own_key, (), max(1, total - limit), min(limit, total - 1) + 1)
        return jnp.stack([one, total - one])
    sizes = jnp.asarray(length_profile(number_of, total, limit, lean), jnp.int32)
    twos = (number_of - 1) // 2
    giver, taker = sizes[1:1 + 2 * twos:2], sizes[2:2 + 2 * twos:2]
    slack = jnp.minimum(giver - 1, limit - taker)
    moved = jax.random.randint(jax.random.fold_in(own_key, 1), (twos,), 0, 1 << 20) % (slack + 1)
    sizes = sizes.at[1:1 + 2 * twos:2].set(giver - moved).at[2:2 + 2 * twos:2].set(taker + moved)
    return sizes[jax.random.permutation(jax.random.fold_in(own_key, 2), number_of)]


def centred(stream_key, extent, width, limit, pieces=(), kind=jnp.bfloat16):
    drawn = width * jax.random.normal(stream_key, extent, jnp.float32)
    if pieces:
        drawn = drawn * shard_levels(stream_key, extent, pieces, -0.22, 0.18)
    return jnp.clip(drawn, -limit, limit).astype(kind)


def setup_inputs(seed: int = 0) -> dict:
    key_list = jax.random.split(jax.random.key(seed), 8)
    return {
        "activations": draw_activations(jax.random.fold_in(key_list[7], 71), 0),
        "w_query": centred(key_list[1], (D, QH * HD), D ** -0.5, 0.0625, ((1, 4),)),
        "w_key": centred(key_list[2], (D, KVH * HD), D ** -0.5, 0.0625, ((1, 4),)),
        "w_value": centred(key_list[3], (D, KVH * HD), D ** -0.5, 0.0625, ((1, 4),)),
        "doc_lengths": ragged(key_list[4], NDOC, TOKENS, TOKENS // 2, 2).astype(jnp.int32),
        "block_dest": draw_block_dest(jax.random.fold_in(key_list[7], 71), 0),
        "out_grad": centred(key_list[6], (TOKENS, QH * HD), 1.0, 6.0, ((0, 8), (1, 4))),
    }


NEG = -1e+30

def layout(block_dest):
    nblk = block_dest.shape[0]
    index = jnp.arange(nblk, dtype=jnp.int32)
    order_key = block_dest.astype(jnp.int32) * nblk + index
    ranks = lax.optimization_barrier(jnp.sum((order_key[None, :] < order_key[:, None]).astype(jnp.int32), axis=1))
    ctx_blocks = lax.optimization_barrier(jnp.sum(jnp.where(ranks[None, :] == index[:, None], index[None, :], 0), axis=1)).astype(jnp.int32)
    ctx_pos = (ctx_blocks[:, None] * BLK + jnp.arange(BLK, dtype=jnp.int32)[None, :]).reshape(-1)
    return (ctx_blocks, ctx_pos)

def doc_ids(positions, doc_lengths):
    ends = jnp.cumsum(doc_lengths.astype(jnp.int32)).astype(jnp.int32)
    return lax.optimization_barrier(jnp.sum((ends[None, :] <= positions[:, None]).astype(jnp.int32), axis=1)).astype(jnp.int32)

def reference(activations, w_query, w_key, w_value, doc_lengths, block_dest, out_grad):
    scale = 1.0 / math.sqrt(HD)
    queries = jnp.dot(activations, w_query, preferred_element_type=jnp.float32).astype(jnp.bfloat16)
    keys = jnp.dot(activations, w_key, preferred_element_type=jnp.float32).astype(jnp.bfloat16)
    values = jnp.dot(activations, w_value, preferred_element_type=jnp.float32).astype(jnp.bfloat16)
    ctx_blocks, ctx_pos = layout(block_dest)
    loader_pos = jnp.arange(TOKENS, dtype=jnp.int32)
    docs = doc_ids(loader_pos, doc_lengths)
    visible = (docs[None, :] == docs[:, None]) & (loader_pos[None, :] <= loader_pos[:, None])
    grad_loader = jnp.zeros_like(out_grad).at[ctx_pos].set(out_grad)
    query_g = queries.reshape(TOKENS, KVH, QPK, HD).transpose(1, 0, 2, 3)
    key_g = keys.reshape(TOKENS, KVH, HD).transpose(1, 0, 2)
    value_g = values.reshape(TOKENS, KVH, HD).transpose(1, 0, 2)
    grad_g = grad_loader.reshape(TOKENS, KVH, QPK, HD).transpose(1, 0, 2, 3)

    def one_group(operands):
        query_h, key_h, value_h, grad_h = operands
        query_f = query_h.astype(jnp.float32)
        key_f = key_h.astype(jnp.float32)
        value_f = value_h.astype(jnp.float32)
        grad_f = grad_h.astype(jnp.float32)
        scores = jnp.einsum('tqe,se->qts', query_f, key_f) * scale
        masked = jnp.where(visible[None], scores, NEG)
        top = lax.optimization_barrier(jnp.max(masked, axis=-1, keepdims=True))
        total = lax.optimization_barrier(jnp.sum(jnp.where(visible[None], jnp.exp(masked - top), 0.0), axis=-1, keepdims=True))
        lse = top + jnp.log(total)
        weights = jnp.where(visible[None], jnp.exp(scores - lse), 0.0)
        weights_b = lax.optimization_barrier(weights.astype(jnp.bfloat16)).astype(jnp.float32)
        attn = jnp.einsum('qts,se->tqe', weights, value_f, precision=lax.Precision.HIGHEST).astype(jnp.bfloat16)
        delta = lax.optimization_barrier(jnp.sum(grad_f * attn.astype(jnp.float32), axis=-1))
        dvalue = jnp.einsum('qts,tqe->se', weights_b, grad_f)
        dprob = jnp.einsum('tqe,se->qts', grad_f, value_f)
        dscore = (weights * (dprob - delta.T[:, :, None]) * scale).astype(jnp.bfloat16)
        dscore_f = lax.optimization_barrier(dscore).astype(jnp.float32)
        dquery = jnp.einsum('qts,se->tqe', dscore_f, key_f)
        dkey = jnp.einsum('qts,tqe->se', dscore_f, query_f)
        return (attn, dquery.astype(jnp.bfloat16), dkey.astype(jnp.bfloat16), dvalue.astype(jnp.bfloat16))
    attn_g, dquery_g, dkey_g, dvalue_g = lax.map(one_group, (query_g, key_g, value_g, grad_g))
    attn_loader = attn_g.transpose(1, 0, 2, 3).reshape(TOKENS, QH * HD)
    attention = attn_loader[ctx_pos]
    dquery = dquery_g.transpose(1, 0, 2, 3).reshape(TOKENS, QH * HD)
    dkey = dkey_g.transpose(1, 0, 2).reshape(TOKENS, KVH * HD)
    dvalue = dvalue_g.transpose(1, 0, 2).reshape(TOKENS, KVH * HD)
    input_grad = jnp.dot(dquery, w_query.T, preferred_element_type=jnp.float32)
    input_grad = input_grad + jnp.dot(dkey, w_key.T, preferred_element_type=jnp.float32)
    input_grad = input_grad + jnp.dot(dvalue, w_value.T, preferred_element_type=jnp.float32)
    return (attention, input_grad.astype(jnp.bfloat16))
```

```python
import functools
import math

import jax
import jax.numpy as jnp
from jax import lax
from jax.experimental import pallas as pl
from jax.experimental.pallas import tpu as pltpu
from jax.sharding import PartitionSpec as P

HD = 128
QPK = 4
NEG = -1e30
BF = jnp.bfloat16
F32 = jnp.float32


def layout(block_dest):
    nblk = block_dest.shape[0]
    index = jnp.arange(nblk, dtype=jnp.int32)
    order_key = block_dest * nblk + index
    ranks = jnp.sum((order_key[None, :] < order_key[:, None]).astype(jnp.int32), axis=1)
    return jnp.sum(jnp.where(ranks[None, :] == index[:, None], index[None, :], 0), axis=1)


def spread(table, array, block_rows):
    width = array.shape[-1]
    grouped = array.reshape(table.shape[1], block_rows * width)
    moved = jnp.dot(table, grouped, preferred_element_type=F32)
    return moved.astype(BF).reshape(table.shape[0], block_rows, width)


def dot_nt(a, b):
    return lax.dot_general(a, b, (((1,), (1,)), ((), ())), preferred_element_type=F32)


def dot_tn(a, b):
    return lax.dot_general(a, b, (((0,), (0,)), ((), ())), preferred_element_type=F32)


def dot_nn(a, b):
    return jnp.dot(a, b, preferred_element_type=F32)


def bias_of(start, rank, keys):
    rows = start.shape[0]
    qpos = rank * rows + lax.broadcasted_iota(jnp.int32, (rows, keys), 0)
    col = lax.broadcasted_iota(jnp.int32, (rows, keys), 1)
    slot = col // rows
    kpos = (rank - 2 * slot) * rows + col
    seen = (kpos <= qpos) & (kpos >= start)
    return jnp.where(seen, 0.0, NEG)


def attend_head(h, q_ref, kv_ref, g_ref, bias_ref, att_ref, dq_ref, dkv_ref, first):
    scale = 1.0 / math.sqrt(HD)
    half = kv_ref.shape[1] // 2
    hs = slice(h * HD, (h + 1) * HD)
    g = h // QPK
    ks = slice(g * HD, (g + 1) * HD)
    vs = slice(half + g * HD, half + (g + 1) * HD)
    q = q_ref[:, hs]
    go = g_ref[:, hs]
    k = kv_ref[:, ks]
    v = kv_ref[:, vs]
    s = dot_nt(q, k) * scale + bias_ref[...]
    m = jnp.max(s, axis=1, keepdims=True)
    p = jnp.exp(s - m)
    w = p * (1.0 / jnp.sum(p, axis=1, keepdims=True))
    wb = w.astype(BF)
    low = (w - wb.astype(F32)).astype(BF)
    att = (dot_nn(wb, v) + dot_nn(low, v)).astype(BF)
    att_ref[:, hs] = att
    delta = jnp.sum(go.astype(F32) * att.astype(F32), axis=1, keepdims=True)
    ds = (w * (dot_nt(go, v) - delta) * scale).astype(BF)
    dq_ref[:, hs] = dot_nn(ds, k).astype(BF)
    dk = dot_tn(ds, q)
    dv = dot_tn(wb, go)
    if first:
        dkv_ref[:, ks] = dk
        dkv_ref[:, vs] = dv
    else:
        dkv_ref[:, ks] += dk
        dkv_ref[:, vs] += dv


def attn_kernel(heads, start_ref, q_ref, kv_ref, g_ref, att_ref, dq_ref, dkv_ref, bias_ref, sum_ref):
    rank = lax.axis_index("ctx")
    bias_ref[...] = bias_of(start_ref[...], rank, kv_ref.shape[0])
    for h in range(heads):
        attend_head(h, q_ref, kv_ref, g_ref, bias_ref, att_ref, dq_ref, sum_ref, h % QPK == 0)
    dkv_ref[...] = sum_ref[...].astype(BF)


def attention(start, q, kv, g):
    keys = kv.shape[0]
    rows, width = q.shape
    vm = pl.BlockSpec(memory_space=pltpu.VMEM)
    return pl.pallas_call(
        functools.partial(attn_kernel, width // HD),
        out_shape=(
            jax.ShapeDtypeStruct((rows, width), BF),
            jax.ShapeDtypeStruct((rows, width), BF),
            jax.ShapeDtypeStruct(kv.shape, BF),
        ),
        in_specs=[vm] * 4,
        out_specs=(vm,) * 3,
        scratch_shapes=[pltpu.VMEM((rows, keys), F32), pltpu.VMEM(kv.shape, F32)],
        compiler_params=pltpu.CompilerParams(vmem_limit_bytes=40 * 2**20),
        name="attention",
    )(start, q, kv, g)


def shift(value, steps):
    count = lax.axis_size("ctx")
    pairs = [(s, s + steps) for s in range(count) if 0 <= s + steps < count]
    return lax.ppermute(value, "ctx", pairs)


def per_device(activations, w_query, w_key, w_value, doc_lengths, block_dest, out_grad):
    ctx_count = lax.axis_size("ctx")
    ctx_rank = lax.axis_index("ctx")
    tok_dev = activations.shape[0]
    nblk = block_dest.shape[0]
    block_rows = tok_dev * ctx_count // nblk
    blocks_here = tok_dev // block_rows
    ctx_blocks = layout(block_dest)
    slots = jnp.arange(ctx_count, dtype=jnp.int32)
    my_dest = lax.dynamic_slice_in_dim(block_dest, ctx_rank * blocks_here, blocks_here, 0)
    send_map = (my_dest[None, :] == slots[:, None]).astype(BF)
    mine = lax.dynamic_slice_in_dim(ctx_blocks, ctx_rank * blocks_here, blocks_here, 0)
    take_map = ((mine // blocks_here)[:, None] == slots[None, :]).astype(BF)
    ends = jnp.cumsum(doc_lengths)
    my_pos = ctx_rank * tok_dev + jnp.arange(tok_dev, dtype=jnp.int32)
    start = jnp.max(jnp.where(ends[None, :] <= my_pos[:, None], ends[None, :], 0), axis=1)[:, None]

    def exchange(table_out, value, table_in):
        sent = lax.all_to_all(
            spread(table_out, value, block_rows), "ctx", split_axis=0, concat_axis=0, tiled=True
        )
        return spread(table_in, sent, block_rows).reshape(tok_dev, -1)

    grad = exchange(take_map.T, out_grad, send_map.T)
    piece = lax.all_gather(activations, "heads", axis=1, tiled=True)
    k = dot_nn(piece, w_key).astype(BF)
    v = dot_nn(piece, w_value).astype(BF)
    kv = jnp.concatenate([k, v], axis=1)
    back = ctx_count // 2
    kvs = jnp.concatenate([kv] + [shift(kv, j) for j in range(1, back + 1)], axis=0)
    q = dot_nn(piece, w_query).astype(BF)
    att, dq, dkvs = attention(start, q, kvs, grad)
    out = exchange(send_map, att, take_map)
    total = dkvs[:tok_dev].astype(F32)
    for j in range(1, back + 1):
        total = total + shift(dkvs[j * tok_dev : (j + 1) * tok_dev], -j).astype(F32)
    dkv = total.astype(BF)
    half = dkv.shape[1] // 2
    terms = dot_nt(dq, w_query) + dot_nt(dkv[:, :half], w_key) + dot_nt(dkv[:, half:], w_value)
    input_grad = lax.psum_scatter(terms.astype(BF), "heads", scatter_dimension=1, tiled=True)
    return (out, input_grad)


def solution(mesh):
    return jax.shard_map(
        per_device,
        mesh=mesh,
        in_specs=(
            P("ctx", "heads"),
            P(None, "heads"),
            P(None, "heads"),
            P(None, "heads"),
            P(),
            P(),
            P("ctx", "heads"),
        ),
        out_specs=(P("ctx", "heads"), P("ctx", "heads")),
        check_vma=False,
    )
```

```python
import math

import jax
import jax.numpy as jnp
from jax import lax
from jax.experimental import pallas as pl
from jax.experimental.pallas import tpu as pltpu
from jax.sharding import PartitionSpec as P

HD = 128
QPK = 4
NEG = -1e30
BF = jnp.bfloat16
F32 = jnp.float32


def layout(block_dest):
    nblk = block_dest.shape[0]
    index = jnp.arange(nblk, dtype=jnp.int32)
    order_key = block_dest * nblk + index
    ranks = jnp.sum((order_key[None, :] < order_key[:, None]).astype(jnp.int32), axis=1)
    return jnp.sum(jnp.where(ranks[None, :] == index[:, None], index[None, :], 0), axis=1)


def spread(table, array, block_rows):
    width = array.shape[-1]
    grouped = array.reshape(table.shape[1], block_rows * width)
    moved = jnp.dot(table, grouped, preferred_element_type=F32)
    return moved.astype(BF).reshape(table.shape[0], block_rows, width)


def dot_nt(a, b):
    return lax.dot_general(a, b, (((1,), (1,)), ((), ())), preferred_element_type=F32)


def dot_tn(a, b):
    return lax.dot_general(a, b, (((0,), (0,)), ((), ())), preferred_element_type=F32)


def dot_nn(a, b):
    return jnp.dot(a, b, preferred_element_type=F32)


def bias_of(start, rank, keys):
    rows = start.shape[0]
    qpos = rank * rows + lax.broadcasted_iota(jnp.int32, (rows, keys), 0)
    col = lax.broadcasted_iota(jnp.int32, (rows, keys), 1)
    slot = col // rows
    kpos = (rank - 2 * slot) * rows + col
    seen = (kpos <= qpos) & (kpos >= start)
    return jnp.where(seen, 0.0, NEG)


def attend_head(h, q_ref, kv_ref, g_ref, bias_ref, att_ref, dq_ref, dkv_ref, first):
    scale = 1.0 / math.sqrt(HD)
    half = kv_ref.shape[1] // 2
    hs = slice(h * HD, (h + 1) * HD)
    g = h // QPK
    ks = slice(g * HD, (g + 1) * HD)
    vs = slice(half + g * HD, half + (g + 1) * HD)
    q = q_ref[:, hs]
    go = g_ref[:, hs]
    k = kv_ref[:, ks]
    v = kv_ref[:, vs]
    s = dot_nt(q, k) * scale + bias_ref[...]
    m = jnp.max(s, axis=1, keepdims=True)
    p = jnp.exp(s - m)
    w = p * (1.0 / jnp.sum(p, axis=1, keepdims=True))
    wb = w.astype(BF)
    low = (w - wb.astype(F32)).astype(BF)
    att = (dot_nn(wb, v) + dot_nn(low, v)).astype(BF)
    att_ref[:, hs] = att
    delta = jnp.sum(go.astype(F32) * att.astype(F32), axis=1, keepdims=True)
    ds = (w * (dot_nt(go, v) - delta) * scale).astype(BF)
    dq_ref[:, hs] = dot_nn(ds, k).astype(BF)
    dk = dot_tn(ds, q)
    dv = dot_tn(wb, go)
    if first:
        dkv_ref[:, :HD] = dk
        dkv_ref[:, HD:] = dv
    else:
        dkv_ref[:, :HD] += dk
        dkv_ref[:, HD:] += dv


def back_kernel(
    start_ref, dest_ref, q_ref, kv_ref, g_ref, wq_hbm, wk_hbm, wv_hbm,
    got_ref, out_ref,
    bias, att, dq, sums, send, xrx, zsend, zrx, own, dk, dv, slots, tq,
    near_tx, near_rx, pre_tx, pre_rx, far_tx, far_rx, wq, wk, wv,
    wsem, xs, xr, zs, zr, asend, arecv, nts, ntr, pts, ptr, fts, ftr,
):
    rank = lax.axis_index("ctx")
    head = lax.axis_index("heads")
    ranks = lax.axis_size("ctx")
    nheads = lax.axis_size("heads")
    chips = nheads // 2
    core = lax.rem(head, 2)
    chip = head // 2
    sib = head + 1 - 2 * core
    side = lax.rem(rank, 2)
    pair = rank // 2
    mate = rank + 1 - 2 * side
    rows = q_ref.shape[0]
    qheads = q_ref.shape[1] // HD
    groups = qheads // QPK
    back = ranks // 2
    reach = back // 2
    chunks = tq.shape[1]
    width = tq.shape[3]
    barrier = pltpu.get_barrier_semaphore()

    def to(ctx, h):
        return dict(device_id=(ctx, h), device_id_type=pl.DeviceIdType.MESH)

    def across(d):
        return lax.rem(chip + d, chips) * 2 + core

    for o in range(1, ranks):
        pl.semaphore_signal(barrier, inc=1, **to(lax.rem(rank + o, ranks), head))
    for d in range(1, chips):
        pl.semaphore_signal(barrier, inc=1, **to(rank, across(d)))
    pl.semaphore_signal(barrier, inc=1, **to(rank, sib))
    loads = [
        pltpu.make_async_copy(s, t, wsem.at[i])
        for i, (s, t) in enumerate(((wq_hbm, wq), (wk_hbm, wk), (wv_hbm, wv)))
    ]
    for load in loads:
        load.start()
    bias[...] = bias_of(start_ref[...], rank, kv_ref.shape[0])

    def xcopy(g, i):
        return pltpu.make_async_remote_copy(
            src_ref=send.at[g, 2 * i + 1],
            dst_ref=xrx.at[g, i + 1],
            send_sem=xs.at[g, i],
            recv_sem=xr.at[g, i],
            **to(mate, head),
        )

    def zcopy(g, d):
        return pltpu.make_async_remote_copy(
            src_ref=zsend.at[g, d - 1],
            dst_ref=zrx.at[g, d - 1],
            send_sem=zs.at[g, d - 1],
            recv_sem=zr.at[g, d - 1],
            **to(rank - 2 * d, head),
        )

    def put_dkv(g):
        send[g] = sums[...].astype(BF).reshape(send.shape[1:])
        for i in reversed(range(reach)):
            xcopy(g, i).start()

    def pass_on(g):
        for i in range(reach):
            xcopy(g, i).wait()
        for d in range(reach, -1, -1):
            both = send[g, 2 * d].astype(F32) + xrx[g, d + 1 - side].astype(F32)
            if d == 0:
                own[g] = both
            else:
                zsend[g, d - 1] = both.astype(BF)

                @pl.when(pair >= d)
                def _():
                    zcopy(g, d).start()

    def collect(g):
        for d in range(1, reach + 1):
            @pl.when(pair >= d)
            def _():
                zcopy(g, d).wait_send()

            @pl.when(pair + d < ranks // 2)
            def _():
                zcopy(g, d).wait_recv()
                own[g] += zrx[g, d - 1].astype(F32)

        total = own[g].astype(BF)
        dk[:, g * HD : (g + 1) * HD] = total[:, :HD]
        dv[:, g * HD : (g + 1) * HD] = total[:, HD:]

    for g in range(groups):
        xrx[g, 0] = jnp.zeros(xrx.shape[2:], BF)
        xrx[g, reach + 1] = jnp.zeros(xrx.shape[2:], BF)
    for g in range(groups):
        for i in range(QPK):
            attend_head(g * QPK + i, q_ref, kv_ref, g_ref, bias, att, dq, sums, i == 0)
            if g > 0 and i == 1:
                pass_on(g - 1)
        if g == 0:
            pl.semaphore_wait(barrier, ranks + chips - 1)
        put_dkv(g)

    for load in loads:
        load.wait()

    def piece(t, c):
        return pl.ds(pl.multiple_of((t * chunks + c) * width, width), width)

    def query_part(t):
        @pl.loop(0, chunks)
        def _(c):
            tq[t, c] = dot_nt(dq[...], wq[piece(t, c), :])

    for d in range(1, chips):
        query_part(across(d) + 1 - 2 * core)
    pass_on(groups - 1)
    nblk = rows // slots.shape[1]
    block = slots.shape[1]

    def acopy(o):
        peer = lax.rem(rank + o, ranks)
        return pltpu.make_async_remote_copy(
            src_ref=slots.at[o],
            dst_ref=got_ref.at[rank],
            send_sem=asend.at[o],
            recv_sem=arecv.at[o],
            **to(peer, head),
        )

    for o in range(ranks):
        target = lax.rem(rank + o, ranks)
        value = jnp.zeros(slots.shape[1:], F32)
        for b in range(nblk):
            part = slice(b * block, (b + 1) * block)
            here = (dest_ref[part, :] == target).astype(F32)
            value = value + att[part, :].astype(F32) * here
        if o == 0:
            got_ref[rank] = value.astype(BF)
        else:
            slots[o] = value.astype(BF)
            acopy(o).start()
    for d in range(1, chips):
        query_part(across(d))
    query_part(sib)
    query_part(head)
    for g in range(groups):
        collect(g)

    def term(t, c):
        at = piece(t, c)
        return tq[t, c] + dot_nt(dk[...], wk[at, :]) + dot_nt(dv[...], wv[at, :])

    def pre(d, c):
        return pltpu.make_async_remote_copy(
            src_ref=pre_tx.at[d - 1, c], dst_ref=pre_rx.at[d - 1, c],
            send_sem=pts.at[d - 1, c], recv_sem=ptr.at[d - 1, c], **to(rank, sib),
        )

    def far(d, c):
        return pltpu.make_async_remote_copy(
            src_ref=far_tx.at[d - 1, c], dst_ref=far_rx.at[d - 1, c],
            send_sem=fts.at[d - 1, c], recv_sem=ftr.at[d - 1, c], **to(rank, across(d)),
        )

    def near(c):
        return pltpu.make_async_remote_copy(
            src_ref=near_tx.at[c], dst_ref=near_rx.at[c],
            send_sem=nts.at[c], recv_sem=ntr.at[c], **to(rank, sib),
        )

    for d in range(1, chips):
        @pl.loop(0, chunks)
        def _(c):
            pre_tx[d - 1, c] = term(across(d) + 1 - 2 * core, c).astype(BF)
            pre(d, c).start()

        @pl.loop(0, chunks)
        def _(c):
            mine = term(across(d), c)
            pre(d, c).wait()
            far_tx[d - 1, c] = (mine + pre_rx[d - 1, c].astype(F32)).astype(BF)
            far(d, c).start()

    @pl.loop(0, chunks)
    def _(c):
        near_tx[c] = term(sib, c).astype(BF)
        near(c).start()

    @pl.loop(0, chunks)
    def _(c):
        tq[head, c] = term(head, c)

    @pl.loop(0, chunks)
    def _(c):
        near(c).wait()
        total = tq[head, c] + near_rx[c].astype(F32)
        for d in range(1, chips):
            far(d, c).wait()
            total = total + far_rx[d - 1, c].astype(F32)
        out_ref[:, pl.ds(pl.multiple_of(c * width, width), width)] = total.astype(BF)

    for o in range(1, ranks):
        acopy(o).wait()


def backward(start, dest, q, kv, g, w_query, w_key, w_value, block_rows):
    ranks = lax.axis_size("ctx")
    nheads = lax.axis_size("heads")
    chips = nheads // 2
    keys = kv.shape[0]
    rows, width = q.shape
    feat = w_query.shape[0] // nheads
    chunks = 4
    cw = feat // chunks
    groups = w_key.shape[1] // HD
    slots = ranks // 2 + 1
    reach = ranks // 4
    vm = pl.BlockSpec(memory_space=pltpu.VMEM)
    hbm = pl.BlockSpec(memory_space=pl.ANY)
    dma = pltpu.SemaphoreType.DMA
    return pl.pallas_call(
        back_kernel,
        out_shape=(
            jax.ShapeDtypeStruct((ranks, block_rows, width), BF),
            jax.ShapeDtypeStruct((rows, feat), BF),
        ),
        in_specs=[vm] * 5 + [hbm] * 3,
        out_specs=(vm, vm),
        scratch_shapes=[
            pltpu.VMEM((rows, keys), F32),
            pltpu.VMEM((rows, width), BF),
            pltpu.VMEM((rows, width), BF),
            pltpu.VMEM((keys, 2 * HD), F32),
            pltpu.VMEM((groups, slots, rows, 2 * HD), BF),
            pltpu.VMEM((groups, reach + 2, rows, 2 * HD), BF),
            pltpu.VMEM((groups, reach, rows, 2 * HD), BF),
            pltpu.VMEM((groups, reach, rows, 2 * HD), BF),
            pltpu.VMEM((groups, rows, 2 * HD), F32),
            pltpu.VMEM((rows, groups * HD), BF),
            pltpu.VMEM((rows, groups * HD), BF),
            pltpu.VMEM((ranks, block_rows, width), BF),
            pltpu.VMEM((nheads, chunks, rows, cw), F32),
            pltpu.VMEM((chunks, rows, cw), BF),
            pltpu.VMEM((chunks, rows, cw), BF),
            pltpu.VMEM((chips - 1, chunks, rows, cw), BF),
            pltpu.VMEM((chips - 1, chunks, rows, cw), BF),
            pltpu.VMEM((chips - 1, chunks, rows, cw), BF),
            pltpu.VMEM((chips - 1, chunks, rows, cw), BF),
            pltpu.VMEM(w_query.shape, BF),
            pltpu.VMEM(w_key.shape, BF),
            pltpu.VMEM(w_value.shape, BF),
            dma((3,)),
            dma((groups, reach)),
            dma((groups, reach)),
            dma((groups, reach)),
            dma((groups, reach)),
            dma((ranks,)),
            dma((ranks,)),
            dma((chunks,)),
            dma((chunks,)),
            dma((chips - 1, chunks)),
            dma((chips - 1, chunks)),
            dma((chips - 1, chunks)),
            dma((chips - 1, chunks)),
        ],
        compiler_params=pltpu.CompilerParams(
            vmem_limit_bytes=62 * 2**20, collective_id=1, has_side_effects=True
        ),
        name="backward",
    )(start, dest, q, kv, g, w_query, w_key, w_value)


def shift(value, steps):
    count = lax.axis_size("ctx")
    pairs = [(s, s + steps) for s in range(count) if 0 <= s + steps < count]
    return lax.ppermute(value, "ctx", pairs)


def per_device(activations, w_query, w_key, w_value, doc_lengths, block_dest, out_grad):
    ctx_count = lax.axis_size("ctx")
    ctx_rank = lax.axis_index("ctx")
    tok_dev = activations.shape[0]
    nblk = block_dest.shape[0]
    block_rows = tok_dev * ctx_count // nblk
    blocks_here = tok_dev // block_rows
    ctx_blocks = layout(block_dest)
    slots = jnp.arange(ctx_count, dtype=jnp.int32)
    my_dest = lax.dynamic_slice_in_dim(block_dest, ctx_rank * blocks_here, blocks_here, 0)
    send_map = (my_dest[None, :] == slots[:, None]).astype(BF)
    mine = lax.dynamic_slice_in_dim(ctx_blocks, ctx_rank * blocks_here, blocks_here, 0)
    take_map = ((mine // blocks_here)[:, None] == slots[None, :]).astype(BF)
    ends = jnp.cumsum(doc_lengths)
    my_pos = ctx_rank * tok_dev + jnp.arange(tok_dev, dtype=jnp.int32)
    start = jnp.max(jnp.where(ends[None, :] <= my_pos[:, None], ends[None, :], 0), axis=1)[:, None]

    def exchange(table_out, value, table_in):
        sent = lax.all_to_all(
            spread(table_out, value, block_rows), "ctx", split_axis=0, concat_axis=0, tiled=True
        )
        return spread(table_in, sent, block_rows).reshape(tok_dev, -1)

    grad = exchange(take_map.T, out_grad, send_map.T)
    piece = lax.all_gather(activations, "heads", axis=1, tiled=True)
    k = dot_nn(piece, w_key).astype(BF)
    v = dot_nn(piece, w_value).astype(BF)
    kv = jnp.concatenate([k, v], axis=1)
    back = ctx_count // 2
    kvs = jnp.concatenate([kv] + [shift(kv, j) for j in range(1, back + 1)], axis=0)
    q = dot_nn(piece, w_query).astype(BF)
    dest = jnp.repeat(my_dest, block_rows)[:, None]
    got, input_grad = backward(
        start, dest, q, kvs, grad, w_query, w_key, w_value, block_rows
    )
    out = spread(take_map, got, block_rows).reshape(tok_dev, -1)
    return (out, input_grad)


def solution(mesh):
    return jax.shard_map(
        per_device,
        mesh=mesh,
        in_specs=(
            P("ctx", "heads"),
            P(None, "heads"),
            P(None, "heads"),
            P(None, "heads"),
            P(),
            P(),
            P("ctx", "heads"),
        ),
        out_specs=(P("ctx", "heads"), P("ctx", "heads")),
        check_vma=False,
    )
```

```python
import math

import jax
import jax.numpy as jnp
from jax import lax
from jax.experimental import pallas as pl
from jax.experimental.pallas import tpu as pltpu
from jax.sharding import PartitionSpec as P

HD = 128
QPK = 4
NEG = -1e30
BF = jnp.bfloat16
F32 = jnp.float32


def layout(block_dest):
    nblk = block_dest.shape[0]
    index = jnp.arange(nblk, dtype=jnp.int32)
    order_key = block_dest * nblk + index
    ranks = jnp.sum((order_key[None, :] < order_key[:, None]).astype(jnp.int32), axis=1)
    return jnp.sum(jnp.where(ranks[None, :] == index[:, None], index[None, :], 0), axis=1)


def spread(table, array, block_rows):
    width = array.shape[-1]
    grouped = array.reshape(table.shape[1], block_rows * width)
    moved = jnp.dot(table, grouped, preferred_element_type=F32)
    return moved.astype(BF).reshape(table.shape[0], block_rows, width)


def dot_nt(a, b):
    return lax.dot_general(a, b, (((1,), (1,)), ((), ())), preferred_element_type=F32)


def dot_tn(a, b):
    return lax.dot_general(a, b, (((0,), (0,)), ((), ())), preferred_element_type=F32)


def dot_nn(a, b):
    return jnp.dot(a, b, preferred_element_type=F32)


def bias_of(start, rank, keys):
    rows = start.shape[0]
    qpos = rank * rows + lax.broadcasted_iota(jnp.int32, (rows, keys), 0)
    col = lax.broadcasted_iota(jnp.int32, (rows, keys), 1)
    slot = col // rows
    kpos = (rank - 2 * slot) * rows + col
    seen = (kpos <= qpos) & (kpos >= start)
    return jnp.where(seen, 0.0, NEG)


def attend_head(h, q_ref, kv_ref, g_ref, bias_ref, att_ref, dq_ref, dkv_ref, first):
    scale = 1.0 / math.sqrt(HD)
    half = kv_ref.shape[1] // 2
    hs = slice(h * HD, (h + 1) * HD)
    g = h // QPK
    ks = slice(g * HD, (g + 1) * HD)
    vs = slice(half + g * HD, half + (g + 1) * HD)
    q = q_ref[:, hs]
    go = g_ref[:, hs]
    k = kv_ref[:, ks]
    v = kv_ref[:, vs]
    s = dot_nt(q, k) * scale + bias_ref[...]
    m = jnp.max(s, axis=1, keepdims=True)
    p = jnp.exp(s - m)
    w = p * (1.0 / jnp.sum(p, axis=1, keepdims=True))
    wb = w.astype(BF)
    low = (w - wb.astype(F32)).astype(BF)
    att = (dot_nn(wb, v) + dot_nn(low, v)).astype(BF)
    att_ref[:, hs] = att
    delta = jnp.sum(go.astype(F32) * att.astype(F32), axis=1, keepdims=True)
    ds = (w * (dot_nt(go, v) - delta) * scale).astype(BF)
    dq_ref[:, hs] = dot_nn(ds, k).astype(BF)
    dk = dot_tn(ds, q)
    dv = dot_tn(wb, go)
    if first:
        dkv_ref[:, :HD] = dk
        dkv_ref[:, HD:] = dv
    else:
        dkv_ref[:, :HD] += dk
        dkv_ref[:, HD:] += dv


def back_kernel(
    start_ref, dest_ref, q_ref, kv_ref, g_ref, wq_hbm, wk_hbm, wv_hbm,
    got_ref, out_ref,
    bias, att, dq, sums, send, xrx, zsend, zrx, own, dk, dv, slots, tq,
    near_tx, near_rx, pre_tx, pre_rx, far_tx, far_rx, wq, wk, wv,
    wsem, xs, xr, zs, zr, asend, arecv, nts, ntr, pts, ptr, fts, ftr,
):
    rank = lax.axis_index("ctx")
    head = lax.axis_index("heads")
    ranks = lax.axis_size("ctx")
    nheads = lax.axis_size("heads")
    chips = nheads // 2
    core = lax.rem(head, 2)
    chip = head // 2
    sib = head + 1 - 2 * core
    side = lax.rem(rank, 2)
    pair = rank // 2
    mate = rank + 1 - 2 * side
    rows = q_ref.shape[0]
    qheads = q_ref.shape[1] // HD
    groups = qheads // QPK
    back = ranks // 2
    reach = back // 2
    chunks = tq.shape[1]
    width = tq.shape[3]
    barrier = pltpu.get_barrier_semaphore()

    def to(ctx, h):
        return dict(device_id=(ctx, h), device_id_type=pl.DeviceIdType.MESH)

    def across(d):
        return lax.rem(chip + d, chips) * 2 + core

    for o in range(1, ranks):
        pl.semaphore_signal(barrier, inc=1, **to(lax.rem(rank + o, ranks), head))
    for d in range(1, chips):
        pl.semaphore_signal(barrier, inc=1, **to(rank, across(d)))
    pl.semaphore_signal(barrier, inc=1, **to(rank, sib))
    loads = [
        pltpu.make_async_copy(s, t, wsem.at[i])
        for i, (s, t) in enumerate(((wq_hbm, wq), (wk_hbm, wk), (wv_hbm, wv)))
    ]
    for load in loads:
        load.start()
    bias[...] = bias_of(start_ref[...], rank, kv_ref.shape[0])

    def xcopy(g, i):
        return pltpu.make_async_remote_copy(
            src_ref=send.at[g, 2 * i + 1],
            dst_ref=xrx.at[g, i + 1],
            send_sem=xs.at[g, i],
            recv_sem=xr.at[g, i],
            **to(mate, head),
        )

    def zcopy(g, d):
        return pltpu.make_async_remote_copy(
            src_ref=zsend.at[g, d - 1],
            dst_ref=zrx.at[g, d - 1],
            send_sem=zs.at[g, d - 1],
            recv_sem=zr.at[g, d - 1],
            **to(rank - 2 * d, head),
        )

    def put_dkv(g):
        send[g] = sums[...].astype(BF).reshape(send.shape[1:])
        for i in reversed(range(reach)):
            xcopy(g, i).start()

    def pass_on(g):
        for i in range(reach):
            xcopy(g, i).wait()
        for d in range(reach, -1, -1):
            both = send[g, 2 * d].astype(F32) + xrx[g, d + 1 - side].astype(F32)
            if d == 0:
                own[g] = both
            else:
                zsend[g, d - 1] = both.astype(BF)

                @pl.when(pair >= d)
                def _():
                    zcopy(g, d).start()

    def collect(g):
        for d in range(1, reach + 1):
            @pl.when(pair >= d)
            def _():
                zcopy(g, d).wait_send()

            @pl.when(pair + d < ranks // 2)
            def _():
                zcopy(g, d).wait_recv()
                own[g] += zrx[g, d - 1].astype(F32)

        total = own[g].astype(BF)
        dk[:, g * HD : (g + 1) * HD] = total[:, :HD]
        dv[:, g * HD : (g + 1) * HD] = total[:, HD:]

    for g in range(groups):
        xrx[g, 0] = jnp.zeros(xrx.shape[2:], BF)
        xrx[g, reach + 1] = jnp.zeros(xrx.shape[2:], BF)
    for g in range(groups):
        for i in range(QPK):
            attend_head(g * QPK + i, q_ref, kv_ref, g_ref, bias, att, dq, sums, i == 0)
            if g > 0 and i == 1:
                pass_on(g - 1)
        if g == 0:
            pl.semaphore_wait(barrier, ranks + chips - 1)
        put_dkv(g)

    for load in loads:
        load.wait()

    def piece(t, c):
        return pl.ds(pl.multiple_of((t * chunks + c) * width, width), width)

    def query_part(t):
        @pl.loop(0, chunks)
        def _(c):
            tq[t, c] = dot_nt(dq[...], wq[piece(t, c), :])

    for d in range(1, chips):
        query_part(across(d) + 1 - 2 * core)
    pass_on(groups - 1)
    nblk = rows // slots.shape[1]
    block = slots.shape[1]

    def acopy(o):
        peer = lax.rem(rank + o, ranks)
        return pltpu.make_async_remote_copy(
            src_ref=slots.at[o],
            dst_ref=got_ref.at[rank],
            send_sem=asend.at[o],
            recv_sem=arecv.at[o],
            **to(peer, head),
        )

    for o in range(ranks):
        target = lax.rem(rank + o, ranks)
        value = jnp.zeros(slots.shape[1:], F32)
        for b in range(nblk):
            part = slice(b * block, (b + 1) * block)
            here = (dest_ref[part, :] == target).astype(F32)
            value = value + att[part, :].astype(F32) * here
        if o == 0:
            got_ref[rank] = value.astype(BF)
        else:
            slots[o] = value.astype(BF)
            acopy(o).start()
    for d in range(1, chips):
        query_part(across(d))
    query_part(sib)
    query_part(head)
    for g in range(groups):
        collect(g)

    def term(t, c):
        at = piece(t, c)
        return tq[t, c] + dot_nt(dk[...], wk[at, :]) + dot_nt(dv[...], wv[at, :])

    def pre(d, c):
        return pltpu.make_async_remote_copy(
            src_ref=pre_tx.at[d - 1, c], dst_ref=pre_rx.at[d - 1, c],
            send_sem=pts.at[d - 1, c], recv_sem=ptr.at[d - 1, c], **to(rank, sib),
        )

    def far(d, c):
        return pltpu.make_async_remote_copy(
            src_ref=far_tx.at[d - 1, c], dst_ref=far_rx.at[d - 1, c],
            send_sem=fts.at[d - 1, c], recv_sem=ftr.at[d - 1, c], **to(rank, across(d)),
        )

    def near(c):
        return pltpu.make_async_remote_copy(
            src_ref=near_tx.at[c], dst_ref=near_rx.at[c],
            send_sem=nts.at[c], recv_sem=ntr.at[c], **to(rank, sib),
        )

    for d in range(1, chips):
        @pl.loop(0, chunks)
        def _(c):
            pre_tx[d - 1, c] = term(across(d) + 1 - 2 * core, c).astype(BF)
            pre(d, c).start()

        @pl.loop(0, chunks)
        def _(c):
            mine = term(across(d), c)
            pre(d, c).wait()
            far_tx[d - 1, c] = (mine + pre_rx[d - 1, c].astype(F32)).astype(BF)
            far(d, c).start()

    @pl.loop(0, chunks)
    def _(c):
        near_tx[c] = term(sib, c).astype(BF)
        near(c).start()

    @pl.loop(0, chunks)
    def _(c):
        tq[head, c] = term(head, c)

    @pl.loop(0, chunks)
    def _(c):
        near(c).wait()
        total = tq[head, c] + near_rx[c].astype(F32)
        for d in range(1, chips):
            far(d, c).wait()
            total = total + far_rx[d - 1, c].astype(F32)
        out_ref[:, pl.ds(pl.multiple_of(c * width, width), width)] = total.astype(BF)

    for o in range(1, ranks):
        acopy(o).wait()


def backward(start, dest, q, kv, g, w_query, w_key, w_value, block_rows):
    ranks = lax.axis_size("ctx")
    nheads = lax.axis_size("heads")
    chips = nheads // 2
    keys = kv.shape[0]
    rows, width = q.shape
    feat = w_query.shape[0] // nheads
    chunks = 4
    cw = feat // chunks
    groups = w_key.shape[1] // HD
    slots = ranks // 2 + 1
    reach = ranks // 4
    vm = pl.BlockSpec(memory_space=pltpu.VMEM)
    hbm = pl.BlockSpec(memory_space=pl.ANY)
    dma = pltpu.SemaphoreType.DMA
    return pl.pallas_call(
        back_kernel,
        out_shape=(
            jax.ShapeDtypeStruct((ranks, block_rows, width), BF),
            jax.ShapeDtypeStruct((rows, feat), BF),
        ),
        in_specs=[vm] * 5 + [hbm] * 3,
        out_specs=(vm, vm),
        scratch_shapes=[
            pltpu.VMEM((rows, keys), F32),
            pltpu.VMEM((rows, width), BF),
            pltpu.VMEM((rows, width), BF),
            pltpu.VMEM((keys, 2 * HD), F32),
            pltpu.VMEM((groups, slots, rows, 2 * HD), BF),
            pltpu.VMEM((groups, reach + 2, rows, 2 * HD), BF),
            pltpu.VMEM((groups, reach, rows, 2 * HD), BF),
            pltpu.VMEM((groups, reach, rows, 2 * HD), BF),
            pltpu.VMEM((groups, rows, 2 * HD), F32),
            pltpu.VMEM((rows, groups * HD), BF),
            pltpu.VMEM((rows, groups * HD), BF),
            pltpu.VMEM((ranks, block_rows, width), BF),
            pltpu.VMEM((nheads, chunks, rows, cw), F32),
            pltpu.VMEM((chunks, rows, cw), BF),
            pltpu.VMEM((chunks, rows, cw), BF),
            pltpu.VMEM((chips - 1, chunks, rows, cw), BF),
            pltpu.VMEM((chips - 1, chunks, rows, cw), BF),
            pltpu.VMEM((chips - 1, chunks, rows, cw), BF),
            pltpu.VMEM((chips - 1, chunks, rows, cw), BF),
            pltpu.VMEM(w_query.shape, BF),
            pltpu.VMEM(w_key.shape, BF),
            pltpu.VMEM(w_value.shape, BF),
            dma((3,)),
            dma((groups, reach)),
            dma((groups, reach)),
            dma((groups, reach)),
            dma((groups, reach)),
            dma((ranks,)),
            dma((ranks,)),
            dma((chunks,)),
            dma((chunks,)),
            dma((chips - 1, chunks)),
            dma((chips - 1, chunks)),
            dma((chips - 1, chunks)),
            dma((chips - 1, chunks)),
        ],
        compiler_params=pltpu.CompilerParams(
            vmem_limit_bytes=62 * 2**20, collective_id=1, has_side_effects=True
        ),
        name="backward",
    )(start, dest, q, kv, g, w_query, w_key, w_value)


def pick(table_ref, wanted, source, block):
    total = None
    for b in range(source.shape[0] // block):
        part = slice(b * block, (b + 1) * block)
        here = (table_ref[part, :] == wanted).astype(F32)
        term = source[part, :].astype(F32) * here
        total = term if total is None else total + term
    return total.astype(BF)


def front_kernel(
    home_ref, dest_ref, x_ref, grad_ref, wq_hbm, wk_hbm, wv_hbm,
    q_ref, kv_ref, g_ref,
    xall, accq, acck, accv, slots, got, wq, wk, wv,
    wsem, ns, nr, fs, fr, gs, gr, asend, arecv, zs, zr, xs, xr,
):
    rank = lax.axis_index("ctx")
    head = lax.axis_index("heads")
    ranks = lax.axis_size("ctx")
    nheads = lax.axis_size("heads")
    chips = nheads // 2
    core = lax.rem(head, 2)
    chip = head // 2
    turn = 1 - 2 * core
    sib = head + turn
    side = lax.rem(rank, 2)
    pair = rank // 2
    mate = rank + 1 - 2 * side
    rows = x_ref.shape[1]
    block = slots.shape[1]
    reach = ranks // 4
    chunks = x_ref.shape[0]
    width = x_ref.shape[2]
    feat = chunks * width
    half = kv_ref.shape[1] // 2
    barrier = pltpu.get_barrier_semaphore()

    def to(ctx, h):
        return dict(device_id=(ctx, h), device_id_type=pl.DeviceIdType.MESH)

    def across(d):
        return lax.rem(chip + d, chips) * 2 + core

    def behind(d):
        return lax.rem(chip + chips - d, chips) * 2 + core

    for o in range(1, ranks):
        pl.semaphore_signal(barrier, inc=1, **to(lax.rem(rank + o, ranks), head))
    for d in range(1, chips):
        pl.semaphore_signal(barrier, inc=1, **to(rank, across(d)))
    pl.semaphore_signal(barrier, inc=1, **to(rank, sib))

    order = [head, sib]
    for d in range(1, chips):
        order = order + [behind(d), behind(d) + turn]

    def loads(n):
        at = pl.ds(pl.multiple_of(order[n] * feat, feat), feat)
        return [
            pltpu.make_async_copy(s.at[at, :], t.at[at, :], wsem.at[n, i])
            for i, (s, t) in enumerate(((wq_hbm, wq), (wk_hbm, wk), (wv_hbm, wv)))
        ]

    for n in range(nheads):
        for load in loads(n):
            load.start()
    pl.semaphore_wait(barrier, ranks + chips - 1)

    def near(c):
        return pltpu.make_async_remote_copy(
            src_ref=x_ref.at[c], dst_ref=xall.at[head, c],
            send_sem=ns.at[c], recv_sem=nr.at[c], **to(rank, sib),
        )

    def far(d, c):
        return pltpu.make_async_remote_copy(
            src_ref=x_ref.at[c], dst_ref=xall.at[head, c],
            send_sem=fs.at[d - 1, c], recv_sem=fr.at[d - 1, c], **to(rank, across(d)),
        )

    def give(d, c):
        return pltpu.make_async_remote_copy(
            src_ref=xall.at[behind(d), c], dst_ref=xall.at[behind(d), c],
            send_sem=gs.at[d - 1, c], recv_sem=gr.at[d - 1, c], **to(rank, sib),
        )

    for d in range(1, chips):
        for c in range(chunks):
            far(d, c).start()
    for c in range(chunks):
        near(c).start()

    def acopy(o):
        return pltpu.make_async_remote_copy(
            src_ref=slots.at[o], dst_ref=got.at[rank],
            send_sem=asend.at[o], recv_sem=arecv.at[o],
            **to(lax.rem(rank + o, ranks), head),
        )

    for o in range(ranks):
        value = pick(home_ref, lax.rem(rank + o, ranks), grad_ref, block)
        if o == 0:
            got[rank] = value
        else:
            slots[o] = value
            acopy(o).start()

    def weights(t, c):
        return pl.ds(pl.multiple_of(t * feat + c * width, width), width)

    def add_kv(x, t, c):
        at = weights(t, c)
        acck[...] += dot_nn(x, wk[at, :])
        accv[...] += dot_nn(x, wv[at, :])

    def add_q(x, t, c):
        accq[...] += dot_nn(x, wq[weights(t, c), :])

    accq[...] = jnp.zeros_like(accq)
    acck[...] = jnp.zeros_like(acck)
    accv[...] = jnp.zeros_like(accv)
    for load in loads(0):
        load.wait()

    @pl.loop(0, chunks)
    def _(c):
        add_kv(x_ref[c], head, c)
        add_q(x_ref[c], head, c)

    for load in loads(1):
        load.wait()

    @pl.loop(0, chunks)
    def _(c):
        near(c).wait()
        add_kv(xall[sib, c], sib, c)
        add_q(xall[sib, c], sib, c)

    for n in range(2, nheads):
        for load in loads(n):
            load.wait()
    for d in range(1, chips):
        one = behind(d)
        two = one + turn

        @pl.loop(0, chunks)
        def _(c):
            far(d, c).wait()
            give(d, c).start()
            add_kv(xall[one, c], one, c)

            @pl.when(c > 0)
            def _():
                add_q(xall[one, c - 1], one, c - 1)
                add_q(xall[two, c - 1], two, c - 1)

            give(d, c).wait()
            add_kv(xall[two, c], two, c)

        if d < chips - 1:
            add_q(xall[one, chunks - 1], one, chunks - 1)
            add_q(xall[two, chunks - 1], two, chunks - 1)

    kv_ref[:rows, :half] = acck[...].astype(BF)
    kv_ref[:rows, half:] = accv[...].astype(BF)

    def slot(j):
        return pl.ds(pl.multiple_of(j * rows, rows), rows)

    def zcopy(d):
        return pltpu.make_async_remote_copy(
            src_ref=kv_ref.at[slot(0), :], dst_ref=kv_ref.at[slot(2 * d), :],
            send_sem=zs.at[d - 1], recv_sem=zr.at[d - 1], **to(rank + 2 * d, head),
        )

    def xcopy(i):
        return pltpu.make_async_remote_copy(
            src_ref=kv_ref.at[slot(2 * (i + side)), :], dst_ref=kv_ref.at[slot(2 * i + 1), :],
            send_sem=xs.at[i], recv_sem=xr.at[i], **to(mate, head),
        )

    for d in range(1, reach + 1):
        @pl.when(pair + d < ranks // 2)
        def _():
            zcopy(d).start()

        @pl.when(pair < d)
        def _():
            kv_ref[slot(2 * d), :] = jnp.zeros((rows, 2 * half), BF)

    @pl.when(side == 0)
    def _():
        xcopy(0).start()

    one = behind(chips - 1)
    add_q(xall[one, chunks - 1], one, chunks - 1)
    add_q(xall[one + turn, chunks - 1], one + turn, chunks - 1)
    q_ref[...] = accq[...].astype(BF)
    for o in range(1, ranks):
        acopy(o).wait()
    for b in range(rows // block):
        part = slice(b * block, (b + 1) * block)
        total = jnp.zeros(slots.shape[1:], F32)
        for s in range(ranks):
            total = total + got[s].astype(F32) * (dest_ref[part, :] == s).astype(F32)
        g_ref[part, :] = total.astype(BF)
    for d in range(1, reach + 1):
        @pl.when(pair >= d)
        def _():
            zcopy(d).wait_recv()

        if d < reach:
            @pl.when(side == 0)
            def _():
                xcopy(d).start()

        @pl.when(side == 1)
        def _():
            xcopy(d - 1).start()

    for i in range(reach):
        xcopy(i).wait()
    for d in range(1, reach + 1):
        @pl.when(pair + d < ranks // 2)
        def _():
            zcopy(d).wait_send()


def front(home, dest, x, grad, w_query, w_key, w_value, block_rows):
    ranks = lax.axis_size("ctx")
    nheads = lax.axis_size("heads")
    chips = nheads // 2
    chunks, rows, cw = x.shape
    width = w_query.shape[1]
    half = w_key.shape[1]
    reach = ranks // 4
    vm = pl.BlockSpec(memory_space=pltpu.VMEM)
    hbm = pl.BlockSpec(memory_space=pl.ANY)
    dma = pltpu.SemaphoreType.DMA
    return pl.pallas_call(
        front_kernel,
        out_shape=(
            jax.ShapeDtypeStruct((rows, width), BF),
            jax.ShapeDtypeStruct(((ranks // 2 + 1) * rows, 2 * half), BF),
            jax.ShapeDtypeStruct((rows, width), BF),
        ),
        in_specs=[vm] * 4 + [hbm] * 3,
        out_specs=(vm,) * 3,
        scratch_shapes=[
            pltpu.VMEM((nheads, chunks, rows, cw), BF),
            pltpu.VMEM((rows, width), F32),
            pltpu.VMEM((rows, half), F32),
            pltpu.VMEM((rows, half), F32),
            pltpu.VMEM((ranks, block_rows, width), BF),
            pltpu.VMEM((ranks, block_rows, width), BF),
            pltpu.VMEM(w_query.shape, BF),
            pltpu.VMEM(w_key.shape, BF),
            pltpu.VMEM(w_value.shape, BF),
            dma((nheads, 3)),
            dma((chunks,)),
            dma((chunks,)),
            dma((chips - 1, chunks)),
            dma((chips - 1, chunks)),
            dma((chips - 1, chunks)),
            dma((chips - 1, chunks)),
            dma((ranks,)),
            dma((ranks,)),
            dma((reach,)),
            dma((reach,)),
            dma((reach,)),
            dma((reach,)),
        ],
        compiler_params=pltpu.CompilerParams(
            vmem_limit_bytes=60 * 2**20, collective_id=2, has_side_effects=True
        ),
        name="front",
    )(home, dest, x, grad, w_query, w_key, w_value)


def per_device(activations, w_query, w_key, w_value, doc_lengths, block_dest, out_grad):
    ctx_count = lax.axis_size("ctx")
    ctx_rank = lax.axis_index("ctx")
    tok_dev = activations.shape[0]
    nblk = block_dest.shape[0]
    block_rows = tok_dev * ctx_count // nblk
    blocks_here = tok_dev // block_rows
    ctx_blocks = layout(block_dest)
    slots = jnp.arange(ctx_count, dtype=jnp.int32)
    my_dest = lax.dynamic_slice_in_dim(block_dest, ctx_rank * blocks_here, blocks_here, 0)
    mine = lax.dynamic_slice_in_dim(ctx_blocks, ctx_rank * blocks_here, blocks_here, 0)
    take_map = ((mine // blocks_here)[:, None] == slots[None, :]).astype(BF)
    ends = jnp.cumsum(doc_lengths)
    my_pos = ctx_rank * tok_dev + jnp.arange(tok_dev, dtype=jnp.int32)
    start = jnp.max(jnp.where(ends[None, :] <= my_pos[:, None], ends[None, :], 0), axis=1)[:, None]

    home = jnp.repeat(mine // blocks_here, block_rows)[:, None]
    dest = jnp.repeat(my_dest, block_rows)[:, None]
    chunks = 4
    x = activations.reshape(tok_dev, chunks, -1).transpose(1, 0, 2)
    q, kvs, grad = front(home, dest, x, out_grad, w_query, w_key, w_value, block_rows)
    got, input_grad = backward(
        start, dest, q, kvs, grad, w_query, w_key, w_value, block_rows
    )
    out = spread(take_map, got, block_rows).reshape(tok_dev, -1)
    return (out, input_grad)


def solution(mesh):
    return jax.shard_map(
        per_device,
        mesh=mesh,
        in_specs=(
            P("ctx", "heads"),
            P(None, "heads"),
            P(None, "heads"),
            P(None, "heads"),
            P(),
            P(),
            P("ctx", "heads"),
        ),
        out_specs=(P("ctx", "heads"), P("ctx", "heads")),
        check_vma=False,
    )
```

```python
import math

import jax
import jax.numpy as jnp
from jax import lax
from jax.experimental import pallas as pl
from jax.experimental.pallas import tpu as pltpu
from jax.sharding import PartitionSpec as P

HD = 128
QPK = 4
NEG = -1e30
BF = jnp.bfloat16
F32 = jnp.float32


def dot_nt(a, b):
    return lax.dot_general(a, b, (((1,), (1,)), ((), ())), preferred_element_type=F32)


def dot_tn(a, b):
    return lax.dot_general(a, b, (((0,), (0,)), ((), ())), preferred_element_type=F32)


def dot_nn(a, b):
    return jnp.dot(a, b, preferred_element_type=F32)


def row_starts(len_ref, rank, rows):
    pos = rank * rows + lax.broadcasted_iota(jnp.int32, (rows, 1), 0)
    start = jnp.zeros((rows, 1), jnp.int32)
    end = 0
    for i in range(len_ref.shape[0]):
        end = end + len_ref[i]
        start = jnp.where(pos >= end, end, start)
    return start


def one_if(cond):
    return jnp.where(cond, 1.0, 0.0)


def arrivals(block_ref, rank, ranks):
    each = block_ref.shape[0] // ranks
    has = []
    for t in range(ranks):
        count = 0
        for k in range(each):
            count = count + jnp.where(block_ref[t * each + k] == rank, 1, 0)
        has.append(count)

    def place(target):
        return sum(jnp.where(t < target, has[t], 0) for t in range(ranks))

    return has, place


def bias_of(start, rank, keys):
    rows = start.shape[0]
    qpos = rank * rows + lax.broadcasted_iota(jnp.int32, (rows, keys), 0)
    col = lax.broadcasted_iota(jnp.int32, (rows, keys), 1)
    slot = col // rows
    kpos = (rank - 2 * slot) * rows + col
    seen = (kpos <= qpos) & (kpos >= start)
    return jnp.where(seen, 0.0, NEG)


def attend_head(h, q_ref, kv_ref, g_ref, bias_ref, att_ref, dq_ref, dkv_ref, first):
    scale = 1.0 / math.sqrt(HD)
    half = kv_ref.shape[1] // 2
    hs = slice(h * HD, (h + 1) * HD)
    g = h // QPK
    ks = slice(g * HD, (g + 1) * HD)
    vs = slice(half + g * HD, half + (g + 1) * HD)
    q = q_ref[:, hs]
    go = g_ref[:, hs]
    k = kv_ref[:, ks]
    v = kv_ref[:, vs]
    s = dot_nt(q, k) * scale + bias_ref[...]
    m = jnp.max(s, axis=1, keepdims=True)
    p = jnp.exp(s - m)
    w = p * (1.0 / jnp.sum(p, axis=1, keepdims=True))
    wb = w.astype(BF)
    low = (w - wb.astype(F32)).astype(BF)
    att = (dot_nn(wb, v) + dot_nn(low, v)).astype(BF)
    att_ref[:, hs] = att
    delta = jnp.sum(go.astype(F32) * att.astype(F32), axis=1, keepdims=True)
    ds = (w * (dot_nt(go, v) - delta) * scale).astype(BF)
    dq_ref[:, hs] = dot_nn(ds, k).astype(BF)
    dk = dot_tn(ds, q)
    dv = dot_tn(wb, go)
    if first:
        dkv_ref[:, :HD] = dk
        dkv_ref[:, HD:] = dv
    else:
        dkv_ref[:, :HD] += dk
        dkv_ref[:, HD:] += dv


def back_kernel(
    block_ref, len_ref, q_ref, kv_ref, g_ref, wq_hbm, wk_hbm, wv_hbm,
    att_ref, out_ref,
    got_ref, bias, att, dq, sums, send, xrx, zsend, zrx, own, dk, dv, slots, tq,
    near_tx, near_rx, pre_tx, pre_rx, far_tx, far_rx, wq, wk, wv,
    wsem, xs, xr, zs, zr, asend, arecv, nts, ntr, pts, ptr, fts, ftr,
):
    rank = lax.axis_index("ctx")
    head = lax.axis_index("heads")
    ranks = lax.axis_size("ctx")
    nheads = lax.axis_size("heads")
    chips = nheads // 2
    core = lax.rem(head, 2)
    chip = head // 2
    sib = head + 1 - 2 * core
    side = lax.rem(rank, 2)
    pair = rank // 2
    mate = rank + 1 - 2 * side
    rows = q_ref.shape[0]
    qheads = q_ref.shape[1] // HD
    groups = qheads // QPK
    back = ranks // 2
    reach = back // 2
    chunks = tq.shape[1]
    width = tq.shape[3]
    barrier = pltpu.get_barrier_semaphore()

    def to(ctx, h):
        return dict(device_id=(ctx, h), device_id_type=pl.DeviceIdType.MESH)

    def across(d):
        return lax.rem(chip + d, chips) * 2 + core

    for o in range(1, ranks):
        pl.semaphore_signal(barrier, inc=1, **to(lax.rem(rank + o, ranks), head))
    for d in range(1, chips):
        pl.semaphore_signal(barrier, inc=1, **to(rank, across(d)))
    pl.semaphore_signal(barrier, inc=1, **to(rank, sib))
    loads = [
        pltpu.make_async_copy(s, t, wsem.at[i])
        for i, (s, t) in enumerate(((wq_hbm, wq), (wk_hbm, wk), (wv_hbm, wv)))
    ]
    for load in loads:
        load.start()
    bias[...] = bias_of(row_starts(len_ref, rank, rows), rank, kv_ref.shape[0])

    def xcopy(g, i):
        return pltpu.make_async_remote_copy(
            src_ref=send.at[g, 2 * i + 1],
            dst_ref=xrx.at[g, i + 1],
            send_sem=xs.at[g, i],
            recv_sem=xr.at[g, i],
            **to(mate, head),
        )

    def zcopy(g, d):
        return pltpu.make_async_remote_copy(
            src_ref=zsend.at[g, d - 1],
            dst_ref=zrx.at[g, d - 1],
            send_sem=zs.at[g, d - 1],
            recv_sem=zr.at[g, d - 1],
            **to(rank - 2 * d, head),
        )

    def put_dkv(g):
        send[g] = sums[...].astype(BF).reshape(send.shape[1:])
        for i in reversed(range(reach)):
            xcopy(g, i).start()

    def pass_on(g):
        for i in range(reach):
            xcopy(g, i).wait()
        for d in range(reach, -1, -1):
            both = send[g, 2 * d].astype(F32) + xrx[g, d + 1 - side].astype(F32)
            if d == 0:
                own[g] = both
            else:
                zsend[g, d - 1] = both.astype(BF)

                @pl.when(pair >= d)
                def _():
                    zcopy(g, d).start()

    def collect(g):
        for d in range(1, reach + 1):
            @pl.when(pair >= d)
            def _():
                zcopy(g, d).wait_send()

            @pl.when(pair + d < ranks // 2)
            def _():
                zcopy(g, d).wait_recv()
                own[g] += zrx[g, d - 1].astype(F32)

        total = own[g].astype(BF)
        dk[:, g * HD : (g + 1) * HD] = total[:, :HD]
        dv[:, g * HD : (g + 1) * HD] = total[:, HD:]

    for g in range(groups):
        xrx[g, 0] = jnp.zeros(xrx.shape[2:], BF)
        xrx[g, reach + 1] = jnp.zeros(xrx.shape[2:], BF)
    for g in range(groups):
        for i in range(QPK):
            attend_head(g * QPK + i, q_ref, kv_ref, g_ref, bias, att, dq, sums, i == 0)
            if g > 0 and i == 1:
                pass_on(g - 1)
        if g == 0:
            pl.semaphore_wait(barrier, ranks + chips - 1)
        put_dkv(g)

    for load in loads:
        load.wait()

    def piece(t, c):
        return pl.ds(pl.multiple_of((t * chunks + c) * width, width), width)

    def query_part(t):
        @pl.loop(0, chunks)
        def _(c):
            tq[t, c] = dot_nt(dq[...], wq[piece(t, c), :])

    for d in range(1, chips):
        query_part(across(d) + 1 - 2 * core)
    pass_on(groups - 1)
    nblk = rows // slots.shape[1]
    block = slots.shape[1]

    def acopy(o):
        peer = lax.rem(rank + o, ranks)
        return pltpu.make_async_remote_copy(
            src_ref=slots.at[o],
            dst_ref=got_ref.at[rank],
            send_sem=asend.at[o],
            recv_sem=arecv.at[o],
            **to(peer, head),
        )

    for o in range(ranks):
        target = lax.rem(rank + o, ranks)
        value = pick(att, block, lambda b: one_if(block_ref[rank * nblk + b] == target))
        if o == 0:
            got_ref[rank] = value
        else:
            slots[o] = value
            acopy(o).start()
    for d in range(1, chips):
        query_part(across(d))
    for g in range(groups):
        collect(g)

    def term(t, c):
        at = piece(t, c)
        return tq[t, c] + dot_nt(dk[...], wk[at, :]) + dot_nt(dv[...], wv[at, :])

    def pre(d, c):
        return pltpu.make_async_remote_copy(
            src_ref=pre_tx.at[d - 1, c], dst_ref=pre_rx.at[d - 1, c],
            send_sem=pts.at[d - 1, c], recv_sem=ptr.at[d - 1, c], **to(rank, sib),
        )

    def far(d, c):
        return pltpu.make_async_remote_copy(
            src_ref=far_tx.at[d - 1, c], dst_ref=far_rx.at[d - 1, c],
            send_sem=fts.at[d - 1, c], recv_sem=ftr.at[d - 1, c], **to(rank, across(d)),
        )

    def near(c):
        return pltpu.make_async_remote_copy(
            src_ref=near_tx.at[c], dst_ref=near_rx.at[c],
            send_sem=nts.at[c], recv_sem=ntr.at[c], **to(rank, sib),
        )

    for d in range(1, chips):
        @pl.loop(0, chunks)
        def _(c):
            pre_tx[d - 1, c] = term(across(d) + 1 - 2 * core, c).astype(BF)
            pre(d, c).start()

        @pl.loop(0, chunks)
        def _(c):
            mine = term(across(d), c)
            pre(d, c).wait()
            far_tx[d - 1, c] = (mine + pre_rx[d - 1, c].astype(F32)).astype(BF)
            far(d, c).start()

    def direct(t, c):
        at = piece(t, c)
        return (
            dot_nt(dq[...], wq[at, :]) + dot_nt(dk[...], wk[at, :]) + dot_nt(dv[...], wv[at, :])
        )

    @pl.loop(0, chunks)
    def _(c):
        near_tx[c] = direct(sib, c).astype(BF)
        near(c).start()

    @pl.loop(0, chunks)
    def _(c):
        tq[head, c] = direct(head, c)

    for o in range(1, ranks):
        acopy(o).wait()
    has, place = arrivals(block_ref, rank, ranks)
    spots = [place(t) for t in range(ranks)]
    for b in range(nblk):
        total = jnp.zeros(slots.shape[1:], F32)
        for t in range(ranks):
            total = total + got_ref[t].astype(F32) * one_if((has[t] > 0) & (spots[t] == b))
        att_ref[b * block : (b + 1) * block, :] = total.astype(BF)

    @pl.loop(0, chunks)
    def _(c):
        near(c).wait()
        total = tq[head, c] + near_rx[c].astype(F32)
        for d in range(1, chips):
            far(d, c).wait()
            total = total + far_rx[d - 1, c].astype(F32)
        out_ref[:, pl.ds(pl.multiple_of(c * width, width), width)] = total.astype(BF)


def backward(block_dest, doc_lengths, q, kv, g, w_query, w_key, w_value, block_rows):
    ranks = lax.axis_size("ctx")
    nheads = lax.axis_size("heads")
    chips = nheads // 2
    keys = kv.shape[0]
    rows, width = q.shape
    feat = w_query.shape[0] // nheads
    chunks = 4
    cw = feat // chunks
    groups = w_key.shape[1] // HD
    slots = ranks // 2 + 1
    reach = ranks // 4
    vm = pl.BlockSpec(memory_space=pltpu.VMEM)
    hbm = pl.BlockSpec(memory_space=pl.ANY)
    dma = pltpu.SemaphoreType.DMA
    return pl.pallas_call(
        back_kernel,
        out_shape=(
            jax.ShapeDtypeStruct((rows, width), BF),
            jax.ShapeDtypeStruct((rows, feat), BF),
        ),
        in_specs=[pl.BlockSpec(memory_space=pltpu.SMEM)] * 2 + [vm] * 3 + [hbm] * 3,
        out_specs=(vm, vm),
        scratch_shapes=[
            pltpu.VMEM((ranks, block_rows, width), BF),
            pltpu.VMEM((rows, keys), F32),
            pltpu.VMEM((rows, width), BF),
            pltpu.VMEM((rows, width), BF),
            pltpu.VMEM((keys, 2 * HD), F32),
            pltpu.VMEM((groups, slots, rows, 2 * HD), BF),
            pltpu.VMEM((groups, reach + 2, rows, 2 * HD), BF),
            pltpu.VMEM((groups, reach, rows, 2 * HD), BF),
            pltpu.VMEM((groups, reach, rows, 2 * HD), BF),
            pltpu.VMEM((groups, rows, 2 * HD), F32),
            pltpu.VMEM((rows, groups * HD), BF),
            pltpu.VMEM((rows, groups * HD), BF),
            pltpu.VMEM((ranks, block_rows, width), BF),
            pltpu.VMEM((nheads, chunks, rows, cw), F32),
            pltpu.VMEM((chunks, rows, cw), BF),
            pltpu.VMEM((chunks, rows, cw), BF),
            pltpu.VMEM((chips - 1, chunks, rows, cw), BF),
            pltpu.VMEM((chips - 1, chunks, rows, cw), BF),
            pltpu.VMEM((chips - 1, chunks, rows, cw), BF),
            pltpu.VMEM((chips - 1, chunks, rows, cw), BF),
            pltpu.VMEM(w_query.shape, BF),
            pltpu.VMEM(w_key.shape, BF),
            pltpu.VMEM(w_value.shape, BF),
            dma((3,)),
            dma((groups, reach)),
            dma((groups, reach)),
            dma((groups, reach)),
            dma((groups, reach)),
            dma((ranks,)),
            dma((ranks,)),
            dma((chunks,)),
            dma((chunks,)),
            dma((chips - 1, chunks)),
            dma((chips - 1, chunks)),
            dma((chips - 1, chunks)),
            dma((chips - 1, chunks)),
        ],
        compiler_params=pltpu.CompilerParams(
            vmem_limit_bytes=62 * 2**20, collective_id=1, has_side_effects=True
        ),
        name="backward",
    )(block_dest, doc_lengths, q, kv, g, w_query, w_key, w_value)


def pick(source, block, wanted):
    total = None
    for b in range(source.shape[0] // block):
        term = source[b * block : (b + 1) * block, :].astype(F32) * wanted(b)
        total = term if total is None else total + term
    return total.astype(BF)


def front_kernel(
    block_ref, x_ref, grad_ref, wq_hbm, wk_hbm, wv_hbm,
    q_ref, kv_ref, g_ref,
    xall, accq, acck, accv, slots, got, wq, wk, wv,
    wsem, ns, nr, fs, fr, gs, gr, asend, arecv, zs, zr, xs, xr,
):
    rank = lax.axis_index("ctx")
    head = lax.axis_index("heads")
    ranks = lax.axis_size("ctx")
    nheads = lax.axis_size("heads")
    chips = nheads // 2
    core = lax.rem(head, 2)
    chip = head // 2
    turn = 1 - 2 * core
    sib = head + turn
    side = lax.rem(rank, 2)
    pair = rank // 2
    mate = rank + 1 - 2 * side
    rows = x_ref.shape[0]
    block = slots.shape[1]
    nblk = rows // block
    reach = ranks // 4
    chunks = xall.shape[1]
    width = xall.shape[3]
    feat = chunks * width
    half = kv_ref.shape[1] // 2
    barrier = pltpu.get_barrier_semaphore()

    def to(ctx, h):
        return dict(device_id=(ctx, h), device_id_type=pl.DeviceIdType.MESH)

    def across(d):
        return lax.rem(chip + d, chips) * 2 + core

    def behind(d):
        return lax.rem(chip + chips - d, chips) * 2 + core

    for o in range(1, ranks):
        pl.semaphore_signal(barrier, inc=1, **to(lax.rem(rank + o, ranks), head))
    for d in range(1, chips):
        pl.semaphore_signal(barrier, inc=1, **to(rank, across(d)))
    pl.semaphore_signal(barrier, inc=1, **to(rank, sib))

    order = [head, sib]
    for d in range(1, chips):
        order = order + [behind(d), behind(d) + turn]

    def loads(n):
        at = pl.ds(pl.multiple_of(order[n] * feat, feat), feat)
        return [
            pltpu.make_async_copy(s.at[at, :], t.at[at, :], wsem.at[n, i])
            for i, (s, t) in enumerate(((wq_hbm, wq), (wk_hbm, wk), (wv_hbm, wv)))
        ]

    for n in range(nheads):
        for load in loads(n):
            load.start()
    pl.semaphore_wait(barrier, ranks + chips - 1)

    def cols(c):
        return pl.ds(pl.multiple_of(c * width, width), width)

    def near(c):
        return pltpu.make_async_remote_copy(
            src_ref=x_ref.at[:, cols(c)], dst_ref=xall.at[head, c],
            send_sem=ns.at[c], recv_sem=nr.at[c], **to(rank, sib),
        )

    def far(d, c):
        return pltpu.make_async_remote_copy(
            src_ref=x_ref.at[:, cols(c)], dst_ref=xall.at[head, c],
            send_sem=fs.at[d - 1, c], recv_sem=fr.at[d - 1, c], **to(rank, across(d)),
        )

    def give(d, c):
        return pltpu.make_async_remote_copy(
            src_ref=xall.at[behind(d), c], dst_ref=xall.at[behind(d), c],
            send_sem=gs.at[d - 1, c], recv_sem=gr.at[d - 1, c], **to(rank, sib),
        )

    for d in range(1, chips):
        for c in range(chunks):
            far(d, c).start()
    for c in range(chunks):
        near(c).start()

    def acopy(o):
        return pltpu.make_async_remote_copy(
            src_ref=slots.at[o], dst_ref=got.at[rank],
            send_sem=asend.at[o], recv_sem=arecv.at[o],
            **to(lax.rem(rank + o, ranks), head),
        )

    has, place = arrivals(block_ref, rank, ranks)
    for o in range(ranks):
        spot = place(lax.rem(rank + o, ranks))
        value = pick(grad_ref, block, lambda b: one_if(spot == b))
        if o == 0:
            got[rank] = value
        else:
            slots[o] = value
            acopy(o).start()

    def weights(t, c):
        return pl.ds(pl.multiple_of(t * feat + c * width, width), width)

    def add_kv(x, t, c):
        at = weights(t, c)
        acck[...] += dot_nn(x, wk[at, :])
        accv[...] += dot_nn(x, wv[at, :])

    def add_q(x, t, c):
        accq[...] += dot_nn(x, wq[weights(t, c), :])

    accq[...] = jnp.zeros_like(accq)
    acck[...] = jnp.zeros_like(acck)
    accv[...] = jnp.zeros_like(accv)
    for load in loads(0):
        load.wait()

    @pl.loop(0, chunks)
    def _(c):
        add_kv(x_ref[:, cols(c)], head, c)
        add_q(x_ref[:, cols(c)], head, c)

    for load in loads(1):
        load.wait()

    @pl.loop(0, chunks)
    def _(c):
        near(c).wait()
        add_kv(xall[sib, c], sib, c)
        add_q(xall[sib, c], sib, c)

    for n in range(2, nheads):
        for load in loads(n):
            load.wait()
    for d in range(1, chips):
        one = behind(d)
        two = one + turn

        @pl.loop(0, chunks)
        def _(c):
            far(d, c).wait()
            give(d, c).start()
            add_kv(xall[one, c], one, c)

            @pl.when(c > 0)
            def _():
                add_q(xall[one, c - 1], one, c - 1)
                add_q(xall[two, c - 1], two, c - 1)

            give(d, c).wait()
            add_kv(xall[two, c], two, c)

        if d < chips - 1:
            add_q(xall[one, chunks - 1], one, chunks - 1)
            add_q(xall[two, chunks - 1], two, chunks - 1)

    kv_ref[:rows, :half] = acck[...].astype(BF)
    kv_ref[:rows, half:] = accv[...].astype(BF)

    def slot(j):
        return pl.ds(pl.multiple_of(j * rows, rows), rows)

    def zcopy(d):
        return pltpu.make_async_remote_copy(
            src_ref=kv_ref.at[slot(0), :], dst_ref=kv_ref.at[slot(2 * d), :],
            send_sem=zs.at[d - 1], recv_sem=zr.at[d - 1], **to(rank + 2 * d, head),
        )

    def xcopy(i):
        return pltpu.make_async_remote_copy(
            src_ref=kv_ref.at[slot(2 * (i + side)), :], dst_ref=kv_ref.at[slot(2 * i + 1), :],
            send_sem=xs.at[i], recv_sem=xr.at[i], **to(mate, head),
        )

    for d in range(1, reach + 1):
        @pl.when(pair + d < ranks // 2)
        def _():
            zcopy(d).start()

        @pl.when(pair < d)
        def _():
            kv_ref[slot(2 * d), :] = jnp.zeros((rows, 2 * half), BF)

    @pl.when(side == 0)
    def _():
        xcopy(0).start()

    one = behind(chips - 1)
    add_q(xall[one, chunks - 1], one, chunks - 1)
    add_q(xall[one + turn, chunks - 1], one + turn, chunks - 1)
    q_ref[...] = accq[...].astype(BF)
    for o in range(1, ranks):
        acopy(o).wait()
    for b in range(nblk):
        target = block_ref[rank * nblk + b]
        total = jnp.zeros(slots.shape[1:], F32)
        for s in range(ranks):
            total = total + got[s].astype(F32) * one_if(target == s)
        g_ref[b * block : (b + 1) * block, :] = total.astype(BF)
    for d in range(1, reach + 1):
        @pl.when(pair >= d)
        def _():
            zcopy(d).wait_recv()

        if d < reach:
            @pl.when(side == 0)
            def _():
                xcopy(d).start()

        @pl.when(side == 1)
        def _():
            xcopy(d - 1).start()

    for i in range(reach):
        xcopy(i).wait()
    for d in range(1, reach + 1):
        @pl.when(pair + d < ranks // 2)
        def _():
            zcopy(d).wait_send()


def front(block_dest, x, grad, w_query, w_key, w_value, block_rows):
    ranks = lax.axis_size("ctx")
    nheads = lax.axis_size("heads")
    chips = nheads // 2
    chunks = 4
    rows = x.shape[0]
    cw = x.shape[1] // chunks
    width = w_query.shape[1]
    half = w_key.shape[1]
    reach = ranks // 4
    vm = pl.BlockSpec(memory_space=pltpu.VMEM)
    hbm = pl.BlockSpec(memory_space=pl.ANY)
    dma = pltpu.SemaphoreType.DMA
    return pl.pallas_call(
        front_kernel,
        out_shape=(
            jax.ShapeDtypeStruct((rows, width), BF),
            jax.ShapeDtypeStruct(((ranks // 2 + 1) * rows, 2 * half), BF),
            jax.ShapeDtypeStruct((rows, width), BF),
        ),
        in_specs=[pl.BlockSpec(memory_space=pltpu.SMEM)] + [vm] * 2 + [hbm] * 3,
        out_specs=(vm,) * 3,
        scratch_shapes=[
            pltpu.VMEM((nheads, chunks, rows, cw), BF),
            pltpu.VMEM((rows, width), F32),
            pltpu.VMEM((rows, half), F32),
            pltpu.VMEM((rows, half), F32),
            pltpu.VMEM((ranks, block_rows, width), BF),
            pltpu.VMEM((ranks, block_rows, width), BF),
            pltpu.VMEM(w_query.shape, BF),
            pltpu.VMEM(w_key.shape, BF),
            pltpu.VMEM(w_value.shape, BF),
            dma((nheads, 3)),
            dma((chunks,)),
            dma((chunks,)),
            dma((chips - 1, chunks)),
            dma((chips - 1, chunks)),
            dma((chips - 1, chunks)),
            dma((chips - 1, chunks)),
            dma((ranks,)),
            dma((ranks,)),
            dma((reach,)),
            dma((reach,)),
            dma((reach,)),
            dma((reach,)),
        ],
        compiler_params=pltpu.CompilerParams(
            vmem_limit_bytes=60 * 2**20, collective_id=2, has_side_effects=True
        ),
        name="front",
    )(block_dest, x, grad, w_query, w_key, w_value)


def per_device(activations, w_query, w_key, w_value, doc_lengths, block_dest, out_grad):
    weights = (w_query, w_key, w_value)
    block_rows = activations.shape[0] * lax.axis_size("ctx") // block_dest.shape[0]
    q, kv, grad = front(block_dest, activations, out_grad, *weights, block_rows)
    return backward(block_dest, doc_lengths, q, kv, grad, *weights, block_rows)


def solution(mesh):
    return jax.shard_map(
        per_device,
        mesh=mesh,
        in_specs=(
            P("ctx", "heads"),
            P(None, "heads"),
            P(None, "heads"),
            P(None, "heads"),
            P(),
            P(),
            P("ctx", "heads"),
        ),
        out_specs=(P("ctx", "heads"), P("ctx", "heads")),
        check_vma=False,
    )
```

```python
import math

import jax
import jax.numpy as jnp
from jax import lax
from jax.experimental import pallas as pl
from jax.experimental.pallas import tpu as pltpu
from jax.sharding import PartitionSpec as P

HD = 128
QPK = 4
NEG = -1e30
BF = jnp.bfloat16
F32 = jnp.float32


def dot_nt(a, b):
    return lax.dot_general(a, b, (((1,), (1,)), ((), ())), preferred_element_type=F32)


def dot_tn(a, b):
    return lax.dot_general(a, b, (((0,), (0,)), ((), ())), preferred_element_type=F32)


def dot_nn(a, b):
    return jnp.dot(a, b, preferred_element_type=F32)


def row_starts(len_ref, rank, rows):
    pos = rank * rows + lax.broadcasted_iota(jnp.int32, (rows, 1), 0)
    start = jnp.zeros((rows, 1), jnp.int32)
    end = 0
    for i in range(len_ref.shape[0]):
        end = end + len_ref[i]
        start = jnp.where(pos >= end, end, start)
    return start


def one_if(cond):
    return jnp.where(cond, 1.0, 0.0)


def arrivals(block_ref, rank, ranks):
    each = block_ref.shape[0] // ranks
    has = []
    for t in range(ranks):
        count = 0
        for k in range(each):
            count = count + jnp.where(block_ref[t * each + k] == rank, 1, 0)
        has.append(count)

    def place(target):
        return sum(jnp.where(t < target, has[t], 0) for t in range(ranks))

    return has, place


def bias_of(start, rank, keys):
    rows = start.shape[0]
    qpos = rank * rows + lax.broadcasted_iota(jnp.int32, (rows, keys), 0)
    col = lax.broadcasted_iota(jnp.int32, (rows, keys), 1)
    slot = col // rows
    kpos = (rank - 2 * slot) * rows + col
    seen = (kpos <= qpos) & (kpos >= start)
    return jnp.where(seen, 0.0, NEG)


def attend_head(h, q_ref, kv_ref, g_ref, bias_ref, att_ref, dq_ref, dkv_ref, first):
    scale = 1.0 / math.sqrt(HD)
    half = kv_ref.shape[1] // 2
    hs = slice(h * HD, (h + 1) * HD)
    g = h // QPK
    ks = slice(g * HD, (g + 1) * HD)
    vs = slice(half + g * HD, half + (g + 1) * HD)
    q = q_ref[:, hs]
    go = g_ref[:, hs]
    k = kv_ref[:, ks]
    v = kv_ref[:, vs]
    s = dot_nt(q, k) * scale + bias_ref[...]
    m = jnp.max(s, axis=1, keepdims=True)
    p = jnp.exp(s - m)
    w = p * (1.0 / jnp.sum(p, axis=1, keepdims=True))
    wb = w.astype(BF)
    low = (w - wb.astype(F32)).astype(BF)
    att = (dot_nn(wb, v) + dot_nn(low, v)).astype(BF)
    att_ref[:, hs] = att
    delta = jnp.sum(go.astype(F32) * att.astype(F32), axis=1, keepdims=True)
    ds = (w * (dot_nt(go, v) - delta) * scale).astype(BF)
    dq_ref[:, hs] = dot_nn(ds, k).astype(BF)
    dk = dot_tn(ds, q)
    dv = dot_tn(wb, go)
    if first:
        dkv_ref[:, :HD] = dk
        dkv_ref[:, HD:] = dv
    else:
        dkv_ref[:, :HD] += dk
        dkv_ref[:, HD:] += dv


def back_kernel(
    block_ref, len_ref, q_ref, kv_ref, g_ref, wq_hbm, wk_hbm, wv_hbm,
    att_ref, out_ref,
    got_ref, bias, att, dq, sums, send, xrx, zsend, zrx, own, dk, dv, slots, tq,
    near_tx, near_rx, pre_tx, pre_rx, far_tx, far_rx, wq, wk, wv,
    wsem, xs, xr, zs, zr, asend, arecv, nts, ntr, pts, ptr, fts, ftr,
):
    rank = lax.axis_index("ctx")
    head = lax.axis_index("heads")
    ranks = lax.axis_size("ctx")
    nheads = lax.axis_size("heads")
    chips = nheads // 2
    core = lax.rem(head, 2)
    chip = head // 2
    sib = head + 1 - 2 * core
    side = lax.rem(rank, 2)
    pair = rank // 2
    mate = rank + 1 - 2 * side
    rows = q_ref.shape[0]
    qheads = q_ref.shape[1] // HD
    groups = qheads // QPK
    back = ranks // 2
    reach = back // 2
    chunks = tq.shape[1]
    width = tq.shape[3]
    barrier = pltpu.get_barrier_semaphore()

    def to(ctx, h):
        return dict(device_id=(ctx, h), device_id_type=pl.DeviceIdType.MESH)

    def across(d):
        return lax.rem(chip + d, chips) * 2 + core

    for o in range(1, ranks):
        pl.semaphore_signal(barrier, inc=1, **to(lax.rem(rank + o, ranks), head))
    for d in range(1, chips):
        pl.semaphore_signal(barrier, inc=1, **to(rank, across(d)))
    pl.semaphore_signal(barrier, inc=1, **to(rank, sib))
    loads = [
        pltpu.make_async_copy(s, t, wsem.at[i])
        for i, (s, t) in enumerate(((wq_hbm, wq), (wk_hbm, wk), (wv_hbm, wv)))
    ]
    for load in loads:
        load.start()
    bias[...] = bias_of(row_starts(len_ref, rank, rows), rank, kv_ref.shape[0])

    def xcopy(g, i):
        return pltpu.make_async_remote_copy(
            src_ref=send.at[g, 2 * i + 1],
            dst_ref=xrx.at[g, i + 1],
            send_sem=xs.at[g, i],
            recv_sem=xr.at[g, i],
            **to(mate, head),
        )

    def zcopy(g, d):
        return pltpu.make_async_remote_copy(
            src_ref=zsend.at[g, d - 1],
            dst_ref=zrx.at[g, d - 1],
            send_sem=zs.at[g, d - 1],
            recv_sem=zr.at[g, d - 1],
            **to(rank - 2 * d, head),
        )

    def put_dkv(g):
        send[g] = sums[...].astype(BF).reshape(send.shape[1:])
        for i in reversed(range(reach)):
            xcopy(g, i).start()

    def pass_on(g):
        for i in range(reach):
            xcopy(g, i).wait()
        for d in range(reach, -1, -1):
            both = send[g, 2 * d].astype(F32) + xrx[g, d + 1 - side].astype(F32)
            if d == 0:
                own[g] = both
            else:
                zsend[g, d - 1] = both.astype(BF)

                @pl.when(pair >= d)
                def _():
                    zcopy(g, d).start()

    def collect(g):
        for d in range(1, reach + 1):
            @pl.when(pair >= d)
            def _():
                zcopy(g, d).wait_send()

            @pl.when(pair + d < ranks // 2)
            def _():
                zcopy(g, d).wait_recv()
                own[g] += zrx[g, d - 1].astype(F32)

        total = own[g].astype(BF)
        dk[:, g * HD : (g + 1) * HD] = total[:, :HD]
        dv[:, g * HD : (g + 1) * HD] = total[:, HD:]

    for g in range(groups):
        xrx[g, 0] = jnp.zeros(xrx.shape[2:], BF)
        xrx[g, reach + 1] = jnp.zeros(xrx.shape[2:], BF)
    for g in range(groups):
        for i in range(QPK):
            attend_head(g * QPK + i, q_ref, kv_ref, g_ref, bias, att, dq, sums, i == 0)
            if g > 0 and i == 1:
                pass_on(g - 1)
        if g == 0:
            pl.semaphore_wait(barrier, ranks + chips - 1)
        put_dkv(g)

    for load in loads:
        load.wait()

    def piece(t, c):
        return pl.ds(pl.multiple_of((t * chunks + c) * width, width), width)

    def query_part(t):
        @pl.loop(0, chunks)
        def _(c):
            tq[t, c] = dot_nt(dq[...], wq[piece(t, c), :])

    for d in range(1, chips):
        query_part(across(d) + 1 - 2 * core)
    pass_on(groups - 1)
    nblk = rows // slots.shape[1]
    block = slots.shape[1]

    def acopy(o):
        peer = lax.rem(rank + o, ranks)
        return pltpu.make_async_remote_copy(
            src_ref=slots.at[o],
            dst_ref=got_ref.at[rank],
            send_sem=asend.at[o],
            recv_sem=arecv.at[o],
            **to(peer, head),
        )

    for o in range(ranks):
        target = lax.rem(rank + o, ranks)
        value = pick(att, block, lambda b: one_if(block_ref[rank * nblk + b] == target))
        if o == 0:
            got_ref[rank] = value
        else:
            slots[o] = value
    for d in range(1, chips):
        query_part(across(d))
    for g in range(groups):
        collect(g)
    for o in range(1, ranks):
        acopy(o).start()

    def term(t, c):
        at = piece(t, c)
        return tq[t, c] + dot_nt(dk[...], wk[at, :]) + dot_nt(dv[...], wv[at, :])

    def pre(d, c):
        return pltpu.make_async_remote_copy(
            src_ref=pre_tx.at[d - 1, c], dst_ref=pre_rx.at[d - 1, c],
            send_sem=pts.at[d - 1, c], recv_sem=ptr.at[d - 1, c], **to(rank, sib),
        )

    def far(d, c):
        return pltpu.make_async_remote_copy(
            src_ref=far_tx.at[d - 1, c], dst_ref=far_rx.at[d - 1, c],
            send_sem=fts.at[d - 1, c], recv_sem=ftr.at[d - 1, c], **to(rank, across(d)),
        )

    def near(c):
        return pltpu.make_async_remote_copy(
            src_ref=near_tx.at[c], dst_ref=near_rx.at[c],
            send_sem=nts.at[c], recv_sem=ntr.at[c], **to(rank, sib),
        )

    for d in range(1, chips):
        @pl.loop(0, chunks)
        def _(c):
            pre_tx[d - 1, c] = term(across(d) + 1 - 2 * core, c).astype(BF)
            pre(d, c).start()

        @pl.loop(0, chunks)
        def _(c):
            mine = term(across(d), c)
            pre(d, c).wait()
            far_tx[d - 1, c] = (mine + pre_rx[d - 1, c].astype(F32)).astype(BF)
            far(d, c).start()

    def direct(t, c):
        at = piece(t, c)
        return (
            dot_nt(dq[...], wq[at, :]) + dot_nt(dk[...], wk[at, :]) + dot_nt(dv[...], wv[at, :])
        )

    @pl.loop(0, chunks)
    def _(c):
        near_tx[c] = direct(sib, c).astype(BF)
        near(c).start()

    @pl.loop(0, chunks)
    def _(c):
        tq[head, c] = direct(head, c)

    for o in range(1, ranks):
        acopy(o).wait()
    has, place = arrivals(block_ref, rank, ranks)
    spots = [place(t) for t in range(ranks)]
    for b in range(nblk):
        total = jnp.zeros(slots.shape[1:], F32)
        for t in range(ranks):
            total = total + got_ref[t].astype(F32) * one_if((has[t] > 0) & (spots[t] == b))
        att_ref[b * block : (b + 1) * block, :] = total.astype(BF)

    @pl.loop(0, chunks)
    def _(c):
        near(c).wait()
        total = tq[head, c] + near_rx[c].astype(F32)
        for d in range(1, chips):
            far(d, c).wait()
            total = total + far_rx[d - 1, c].astype(F32)
        out_ref[:, pl.ds(pl.multiple_of(c * width, width), width)] = total.astype(BF)


def backward(block_dest, doc_lengths, q, kv, g, w_query, w_key, w_value, block_rows):
    ranks = lax.axis_size("ctx")
    nheads = lax.axis_size("heads")
    chips = nheads // 2
    keys = kv.shape[0]
    rows, width = q.shape
    feat = w_query.shape[0] // nheads
    chunks = 4
    cw = feat // chunks
    groups = w_key.shape[1] // HD
    slots = ranks // 2 + 1
    reach = ranks // 4
    vm = pl.BlockSpec(memory_space=pltpu.VMEM)
    hbm = pl.BlockSpec(memory_space=pl.ANY)
    dma = pltpu.SemaphoreType.DMA
    return pl.pallas_call(
        back_kernel,
        out_shape=(
            jax.ShapeDtypeStruct((rows, width), BF),
            jax.ShapeDtypeStruct((rows, feat), BF),
        ),
        in_specs=[pl.BlockSpec(memory_space=pltpu.SMEM)] * 2 + [vm] * 3 + [hbm] * 3,
        out_specs=(vm, vm),
        scratch_shapes=[
            pltpu.VMEM((ranks, block_rows, width), BF),
            pltpu.VMEM((rows, keys), F32),
            pltpu.VMEM((rows, width), BF),
            pltpu.VMEM((rows, width), BF),
            pltpu.VMEM((keys, 2 * HD), F32),
            pltpu.VMEM((groups, slots, rows, 2 * HD), BF),
            pltpu.VMEM((groups, reach + 2, rows, 2 * HD), BF),
            pltpu.VMEM((groups, reach, rows, 2 * HD), BF),
            pltpu.VMEM((groups, reach, rows, 2 * HD), BF),
            pltpu.VMEM((groups, rows, 2 * HD), F32),
            pltpu.VMEM((rows, groups * HD), BF),
            pltpu.VMEM((rows, groups * HD), BF),
            pltpu.VMEM((ranks, block_rows, width), BF),
            pltpu.VMEM((nheads, chunks, rows, cw), F32),
            pltpu.VMEM((chunks, rows, cw), BF),
            pltpu.VMEM((chunks, rows, cw), BF),
            pltpu.VMEM((chips - 1, chunks, rows, cw), BF),
            pltpu.VMEM((chips - 1, chunks, rows, cw), BF),
            pltpu.VMEM((chips - 1, chunks, rows, cw), BF),
            pltpu.VMEM((chips - 1, chunks, rows, cw), BF),
            pltpu.VMEM(w_query.shape, BF),
            pltpu.VMEM(w_key.shape, BF),
            pltpu.VMEM(w_value.shape, BF),
            dma((3,)),
            dma((groups, reach)),
            dma((groups, reach)),
            dma((groups, reach)),
            dma((groups, reach)),
            dma((ranks,)),
            dma((ranks,)),
            dma((chunks,)),
            dma((chunks,)),
            dma((chips - 1, chunks)),
            dma((chips - 1, chunks)),
            dma((chips - 1, chunks)),
            dma((chips - 1, chunks)),
        ],
        compiler_params=pltpu.CompilerParams(
            vmem_limit_bytes=62 * 2**20, collective_id=1, has_side_effects=True
        ),
        name="backward",
    )(block_dest, doc_lengths, q, kv, g, w_query, w_key, w_value)


def pick(source, block, wanted):
    total = None
    for b in range(source.shape[0] // block):
        term = source[b * block : (b + 1) * block, :].astype(F32) * wanted(b)
        total = term if total is None else total + term
    return total.astype(BF)


def front_kernel(
    block_ref, x_ref, grad_ref, wq_hbm, wk_hbm, wv_hbm,
    q_ref, kv_ref, g_ref,
    xall, accq, acck, accv, slots, got, wq, wk, wv,
    wsem, ns, nr, fs, fr, gs, gr, asend, arecv, zs, zr, xs, xr,
):
    rank = lax.axis_index("ctx")
    head = lax.axis_index("heads")
    ranks = lax.axis_size("ctx")
    nheads = lax.axis_size("heads")
    chips = nheads // 2
    core = lax.rem(head, 2)
    chip = head // 2
    turn = 1 - 2 * core
    sib = head + turn
    side = lax.rem(rank, 2)
    pair = rank // 2
    mate = rank + 1 - 2 * side
    rows = x_ref.shape[0]
    block = slots.shape[1]
    nblk = rows // block
    reach = ranks // 4
    chunks = xall.shape[1]
    width = xall.shape[3]
    feat = chunks * width
    half = kv_ref.shape[1] // 2
    barrier = pltpu.get_barrier_semaphore()

    def to(ctx, h):
        return dict(device_id=(ctx, h), device_id_type=pl.DeviceIdType.MESH)

    def across(d):
        return lax.rem(chip + d, chips) * 2 + core

    def behind(d):
        return lax.rem(chip + chips - d, chips) * 2 + core

    for o in range(1, ranks):
        pl.semaphore_signal(barrier, inc=1, **to(lax.rem(rank + o, ranks), head))
    for d in range(1, chips):
        pl.semaphore_signal(barrier, inc=1, **to(rank, across(d)))
    pl.semaphore_signal(barrier, inc=1, **to(rank, sib))

    order = [head, sib]
    for d in range(1, chips):
        order = order + [behind(d), behind(d) + turn]

    def loads(n):
        at = pl.ds(pl.multiple_of(order[n] * feat, feat), feat)
        return [
            pltpu.make_async_copy(s.at[at, :], t.at[at, :], wsem.at[n, i])
            for i, (s, t) in enumerate(((wq_hbm, wq), (wk_hbm, wk), (wv_hbm, wv)))
        ]

    for n in range(nheads):
        for load in loads(n):
            load.start()
    pl.semaphore_wait(barrier, ranks + chips - 1)

    def cols(c):
        return pl.ds(pl.multiple_of(c * width, width), width)

    def near(c):
        return pltpu.make_async_remote_copy(
            src_ref=x_ref.at[:, cols(c)], dst_ref=xall.at[head, c],
            send_sem=ns.at[c], recv_sem=nr.at[c], **to(rank, sib),
        )

    def far(d, c):
        return pltpu.make_async_remote_copy(
            src_ref=x_ref.at[:, cols(c)], dst_ref=xall.at[head, c],
            send_sem=fs.at[d - 1, c], recv_sem=fr.at[d - 1, c], **to(rank, across(d)),
        )

    def give(d, c):
        return pltpu.make_async_remote_copy(
            src_ref=xall.at[behind(d), c], dst_ref=xall.at[behind(d), c],
            send_sem=gs.at[d - 1, c], recv_sem=gr.at[d - 1, c], **to(rank, sib),
        )

    for d in range(1, chips):
        for c in range(chunks):
            far(d, c).start()
    for c in range(chunks):
        near(c).start()

    def acopy(o):
        return pltpu.make_async_remote_copy(
            src_ref=slots.at[o], dst_ref=got.at[rank],
            send_sem=asend.at[o], recv_sem=arecv.at[o],
            **to(lax.rem(rank + o, ranks), head),
        )

    has, place = arrivals(block_ref, rank, ranks)
    for o in range(ranks):
        spot = place(lax.rem(rank + o, ranks))
        value = pick(grad_ref, block, lambda b: one_if(spot == b))
        if o == 0:
            got[rank] = value
        else:
            slots[o] = value
            acopy(o).start()

    def weights(t, c):
        return pl.ds(pl.multiple_of(t * feat + c * width, width), width)

    def add_kv(x, t, c):
        at = weights(t, c)
        acck[...] += dot_nn(x, wk[at, :])
        accv[...] += dot_nn(x, wv[at, :])

    def add_q(x, t, c):
        accq[...] += dot_nn(x, wq[weights(t, c), :])

    accq[...] = jnp.zeros_like(accq)
    acck[...] = jnp.zeros_like(acck)
    accv[...] = jnp.zeros_like(accv)
    for load in loads(0):
        load.wait()

    @pl.loop(0, chunks)
    def _(c):
        add_kv(x_ref[:, cols(c)], head, c)
        add_q(x_ref[:, cols(c)], head, c)

    for load in loads(1):
        load.wait()

    @pl.loop(0, chunks)
    def _(c):
        near(c).wait()
        add_kv(xall[sib, c], sib, c)
        add_q(xall[sib, c], sib, c)

    for n in range(2, nheads):
        for load in loads(n):
            load.wait()
    for d in range(1, chips):
        one = behind(d)
        two = one + turn

        @pl.loop(0, chunks)
        def _(c):
            far(d, c).wait()
            give(d, c).start()
            add_kv(xall[one, c], one, c)

            @pl.when(c > 0)
            def _():
                add_q(xall[one, c - 1], one, c - 1)
                add_q(xall[two, c - 1], two, c - 1)

            give(d, c).wait()
            add_kv(xall[two, c], two, c)

        if d < chips - 1:
            add_q(xall[one, chunks - 1], one, chunks - 1)
            add_q(xall[two, chunks - 1], two, chunks - 1)

    kv_ref[:rows, :half] = acck[...].astype(BF)
    kv_ref[:rows, half:] = accv[...].astype(BF)

    def slot(j):
        return pl.ds(pl.multiple_of(j * rows, rows), rows)

    def zcopy(d):
        return pltpu.make_async_remote_copy(
            src_ref=kv_ref.at[slot(0), :], dst_ref=kv_ref.at[slot(2 * d), :],
            send_sem=zs.at[d - 1], recv_sem=zr.at[d - 1], **to(rank + 2 * d, head),
        )

    def xcopy(i):
        return pltpu.make_async_remote_copy(
            src_ref=kv_ref.at[slot(2 * (i + side)), :], dst_ref=kv_ref.at[slot(2 * i + 1), :],
            send_sem=xs.at[i], recv_sem=xr.at[i], **to(mate, head),
        )

    for d in range(1, reach + 1):
        @pl.when(pair + d < ranks // 2)
        def _():
            zcopy(d).start()

        @pl.when(pair < d)
        def _():
            kv_ref[slot(2 * d), :] = jnp.zeros((rows, 2 * half), BF)

    @pl.when(side == 0)
    def _():
        xcopy(0).start()

    one = behind(chips - 1)
    add_q(xall[one, chunks - 1], one, chunks - 1)
    add_q(xall[one + turn, chunks - 1], one + turn, chunks - 1)
    q_ref[...] = accq[...].astype(BF)
    for o in range(1, ranks):
        acopy(o).wait()
    for b in range(nblk):
        target = block_ref[rank * nblk + b]
        total = jnp.zeros(slots.shape[1:], F32)
        for s in range(ranks):
            total = total + got[s].astype(F32) * one_if(target == s)
        g_ref[b * block : (b + 1) * block, :] = total.astype(BF)
    for d in range(1, reach + 1):
        @pl.when(pair >= d)
        def _():
            zcopy(d).wait_recv()

        if d < reach:
            @pl.when(side == 0)
            def _():
                xcopy(d).start()

        @pl.when(side == 1)
        def _():
            xcopy(d - 1).start()

    for i in range(reach):
        xcopy(i).wait()
    for d in range(1, reach + 1):
        @pl.when(pair + d < ranks // 2)
        def _():
            zcopy(d).wait_send()


def front(block_dest, x, grad, w_query, w_key, w_value, block_rows):
    ranks = lax.axis_size("ctx")
    nheads = lax.axis_size("heads")
    chips = nheads // 2
    chunks = 4
    rows = x.shape[0]
    cw = x.shape[1] // chunks
    width = w_query.shape[1]
    half = w_key.shape[1]
    reach = ranks // 4
    vm = pl.BlockSpec(memory_space=pltpu.VMEM)
    hbm = pl.BlockSpec(memory_space=pl.ANY)
    dma = pltpu.SemaphoreType.DMA
    return pl.pallas_call(
        front_kernel,
        out_shape=(
            jax.ShapeDtypeStruct((rows, width), BF),
            jax.ShapeDtypeStruct(((ranks // 2 + 1) * rows, 2 * half), BF),
            jax.ShapeDtypeStruct((rows, width), BF),
        ),
        in_specs=[pl.BlockSpec(memory_space=pltpu.SMEM)] + [vm] * 2 + [hbm] * 3,
        out_specs=(vm,) * 3,
        scratch_shapes=[
            pltpu.VMEM((nheads, chunks, rows, cw), BF),
            pltpu.VMEM((rows, width), F32),
            pltpu.VMEM((rows, half), F32),
            pltpu.VMEM((rows, half), F32),
            pltpu.VMEM((ranks, block_rows, width), BF),
            pltpu.VMEM((ranks, block_rows, width), BF),
            pltpu.VMEM(w_query.shape, BF),
            pltpu.VMEM(w_key.shape, BF),
            pltpu.VMEM(w_value.shape, BF),
            dma((nheads, 3)),
            dma((chunks,)),
            dma((chunks,)),
            dma((chips - 1, chunks)),
            dma((chips - 1, chunks)),
            dma((chips - 1, chunks)),
            dma((chips - 1, chunks)),
            dma((ranks,)),
            dma((ranks,)),
            dma((reach,)),
            dma((reach,)),
            dma((reach,)),
            dma((reach,)),
        ],
        compiler_params=pltpu.CompilerParams(
            vmem_limit_bytes=60 * 2**20, collective_id=2, has_side_effects=True
        ),
        name="front",
    )(block_dest, x, grad, w_query, w_key, w_value)


def per_device(activations, w_query, w_key, w_value, doc_lengths, block_dest, out_grad):
    weights = (w_query, w_key, w_value)
    block_rows = activations.shape[0] * lax.axis_size("ctx") // block_dest.shape[0]
    q, kv, grad = front(block_dest, activations, out_grad, *weights, block_rows)
    return backward(block_dest, doc_lengths, q, kv, grad, *weights, block_rows)


def solution(mesh):
    return jax.shard_map(
        per_device,
        mesh=mesh,
        in_specs=(
            P("ctx", "heads"),
            P(None, "heads"),
            P(None, "heads"),
            P(None, "heads"),
            P(),
            P(),
            P("ctx", "heads"),
        ),
        out_specs=(P("ctx", "heads"), P("ctx", "heads")),
        check_vma=False,
    )
```
